32 devices in a mesh: azim: 8 (over z, y), row: 4 (over x, core).
Axes of the slice: x: 2, y: 2, z: 4, core: 2. Of those that a mesh axis runs over, the one named last changes fastest.
Arguments:
- flow_state: float32 [6, 4, 16, 1024], P(None, None, 'row', 'azim'), may hold values from -6 to 6
- old_state: float32 [6, 4, 16, 1024], P(None, None, 'row', 'azim'), may hold values from -6 to 6
- local_step: float32 [4, 16, 1024], P(None, 'row', 'azim'), may hold values from 0.2 to 2
- azim_flux: float32 [6, 6], replicated, may hold values from -2.5 to 2.5
- axial_flux: float32 [6, 6], replicated, may hold values from -2.5 to 2.5
- block_inverse: float32 [6, 6, 4, 16, 1024], P(None, None, None, 'row', 'azim'), may hold values from -1 to 1
- lower_block: float32 [6, 6, 4, 16, 1024], P(None, None, None, 'row', 'azim')
- intersection_first: int32 [4, 1024], P('row', 'azim'), may hold values from 0 to 1023, as said below
- intersection_weight: int32 [4, 1024], P('row', 'azim'), may hold values from 0 to 7
Outputs:
- new_state: float32 [6, 4, 16, 1024], P(None, None, 'row', 'azim')
The draws below stay inside these ranges and needn't reach their ends.
Inputs may be any that keep to these rules, and one draw needn't show every extreme that they name: In each row r, intersection_first[r, a] = (a + o_r) mod 1024 for one offset o_r of that row.
All inputs are finite; a program needn't handle non-finite values.
Results may differ from the reference program's by a relative error of at most 0.0003.
Values sent between devices are 32-bit elements; how exact they have to be, the bound alone decides.
No kernel may reach another device: no remote copies, remote signals or barrier semaphores. Data moves between devices by JAX's collectives and lax.ppermute only.
A program may use at most 128 MiB of HBM per device.

```python
import math
import jax
import jax.numpy as jnp
from jax import lax

FIELDS = 6
SPANWISE_TOTAL = 4
AXIAL_DEV = 4
STREAMWISE_TOTAL = 16
CIRCUMFER_TOTAL = 1024
N_ROW = 4


def line_rates(key):
    starting_displacement = jax.random.fold_in(key, 11)
    rate_key = jax.random.fold_in(starting_displacement, 1)
    stochastic_gust_seed = jax.random.fold_in(starting_displacement, 2)
    logs = jax.random.uniform(rate_key, (SPANWISE_TOTAL, STREAMWISE_TOTAL), jnp.float32, jnp.log(0.3), jnp.log(CIRCUMFER_TOTAL / 40.0))
    strength = jnp.exp(logs)
    gust_occurrences = jax.random.randint(stochastic_gust_seed, (2, SPANWISE_TOTAL, STREAMWISE_TOTAL), 0, CIRCUMFER_TOTAL)
    vane_locations = jnp.arange(CIRCUMFER_TOTAL, dtype=jnp.int32)
    impacted_volumes = (vane_locations == gust_occurrences[0][..., None]) | (vane_locations == gust_occurrences[1][..., None])
    return strength[..., None] / CIRCUMFER_TOTAL + jnp.where(impacted_volumes, 0.5108256, 0.0)


def plane_block(angles, pairs):
    cosine = jnp.cos(angles)
    sine = jnp.sin(angles)
    matrix = jnp.zeros((6, 6) + angles.shape[1:], jnp.float32)
    for place, pair in enumerate(pairs):
        first_at, second_at = pair
        matrix = matrix.at[first_at, first_at].set(cosine[place])
        matrix = matrix.at[first_at, second_at].set(-sine[place])
        matrix = matrix.at[second_at, first_at].set(sine[place])
        matrix = matrix.at[second_at, second_at].set(cosine[place])
    return matrix


def rotation(key):
    angles = jax.random.uniform(key, (6, SPANWISE_TOTAL, STREAMWISE_TOTAL, CIRCUMFER_TOTAL), jnp.float32, -jnp.pi, jnp.pi)
    inner = plane_block(angles[0:3], ((0, 1), (2, 3), (4, 5)))
    outer = plane_block(angles[3:6], ((1, 2), (3, 4), (5, 0)))
    return jnp.einsum('fg...,gh...->fh...', outer, inner, precision=lax.Precision.HIGHEST)


def draw_block_inverse(key, part):
    rates = line_rates(key)
    scale = jnp.sqrt(-jnp.expm1(-2.0 * rates))
    return scale[None, None] * rotation(jax.random.fold_in(key, 21))


def draw_lower_block(key, part):
    rates = line_rates(key)
    scale = jnp.sqrt(-jnp.expm1(-2.0 * rates))
    retain = jnp.exp(-rates)
    return (retain / scale)[None, None] * rotation(jax.random.fold_in(key, 22))


def draw_intersection_first(key, part):
    offsets = jax.random.randint(jax.random.fold_in(key, 31), (N_ROW, 1), 0, CIRCUMFER_TOTAL)
    vane_locations = jnp.arange(CIRCUMFER_TOTAL, dtype=jnp.int32)[None, :]
    return ((vane_locations + offsets) % CIRCUMFER_TOTAL).astype(jnp.int32)


def plant(values, key, smallest, top_value):
    spot = [jax.random.randint(jax.random.fold_in(key, axis), (), 0, length) for axis, length in enumerate(values.shape)]
    widest = values.shape.index(max(values.shape))
    next_to = spot[:widest] + [(spot[widest] + 1) % values.shape[widest]] + spot[widest + 1:]
    return values.at[tuple(spot)].set(smallest).at[tuple(next_to)].set(top_value)


def shard_levels(rng, extent, split, low, high):
    factor_of = 1.0
    for dim, parts in split:
        draws = jax.random.uniform(jax.random.fold_in(jax.random.fold_in(rng, 6), dim), (parts,), jnp.float32, low / len(split), high / len(split))
        factor_of = factor_of * jnp.repeat(jnp.exp(draws), extent[dim] // parts).reshape((-1,) + (1,) * (len(extent) - 1 - dim))
    return factor_of


def scatter_about(stream_key, shape, deviation, limit, cuts=(), kind=jnp.bfloat16):
    values = deviation * jax.random.normal(stream_key, shape, jnp.float32)
    if cuts:
        values = values * shard_levels(stream_key, shape, cuts, -0.22, 0.18)
    return jnp.clip(values, -limit, limit).astype(kind)


def setup_inputs(seed: int = 0) -> dict:
    seeds = jax.random.split(jax.random.key(seed), 10)
    return {
        "flow_state": scatter_about(seeds[0], (FIELDS, SPANWISE_TOTAL, STREAMWISE_TOTAL, CIRCUMFER_TOTAL), 1.0, 6.0, ((2, 4), (3, 8)), jnp.float32),
        "old_state": scatter_about(seeds[1], (FIELDS, SPANWISE_TOTAL, STREAMWISE_TOTAL, CIRCUMFER_TOTAL), 1.0, 6.0, ((2, 4), (3, 8)), jnp.float32),
        "local_step": jnp.clip(jnp.exp(math.log(2.0) - 2.3025851 * jax.random.uniform(seeds[2], (SPANWISE_TOTAL, STREAMWISE_TOTAL, CIRCUMFER_TOTAL), jnp.float32) ** shard_levels(seeds[2], (SPANWISE_TOTAL, STREAMWISE_TOTAL, CIRCUMFER_TOTAL), ((1, 4), (2, 8)), -0.2, 0.2)), 0.2, 2.0),
        "azim_flux": scatter_about(seeds[3], (FIELDS, FIELDS), FIELDS ** -0.5, 2.5, (), jnp.float32),
        "axial_flux": scatter_about(seeds[4], (FIELDS, FIELDS), FIELDS ** -0.5, 2.5, (), jnp.float32),
        "block_inverse": draw_block_inverse(jax.random.fold_in(seeds[9], 71), 0),
        "lower_block": draw_lower_block(jax.random.fold_in(seeds[9], 71), 0),
        "intersection_first": draw_intersection_first(jax.random.fold_in(seeds[9], 71), 0),
        "intersection_weight": plant(jax.random.randint(seeds[8], (N_ROW, CIRCUMFER_TOTAL), 0, 8), jax.random.fold_in(seeds[8], 1), 0, 7).astype(jnp.int32),
    }


JST_SECOND = 0.5
JST_FOURTH = 1.0 / 32.0
TIME_FACTOR = 1.5

def slice_axis(array, start, stop, axis):
    return lax.slice_in_dim(array, start, stop, axis=axis)

def jst_residual(padded, flux_matrix, axis):
    interior = padded.shape[axis] - 4
    flux_terms = jnp.einsum('fg,g...->f...', flux_matrix, padded, precision=lax.Precision.HIGHEST)
    central = 0.5 * (slice_axis(flux_terms, 3, interior + 3, axis) - slice_axis(flux_terms, 1, interior + 1, axis))
    pressure = 1.0 + padded[0] * padded[0]
    paxis = axis - 1
    press_up = slice_axis(pressure, 2, interior + 4, paxis)
    press_mid = slice_axis(pressure, 1, interior + 3, paxis)
    press_down = slice_axis(pressure, 0, interior + 2, paxis)
    sensor = jnp.abs(press_up - 2.0 * press_mid + press_down) / (press_up + 2.0 * press_mid + press_down)
    left_sensor = slice_axis(sensor, 0, interior + 1, paxis)
    right_sensor = slice_axis(sensor, 1, interior + 2, paxis)
    second = JST_SECOND * jnp.maximum(left_sensor, right_sensor)
    fourth = jnp.maximum(0.0, JST_FOURTH - second)
    behind = slice_axis(padded, 0, interior + 1, axis)
    here_cell = slice_axis(padded, 1, interior + 2, axis)
    ahead = slice_axis(padded, 2, interior + 3, axis)
    beyond = slice_axis(padded, 3, interior + 4, axis)
    face = second[None] * (ahead - here_cell) - fourth[None] * (beyond - 3.0 * ahead + 3.0 * here_cell - behind)
    return central - (slice_axis(face, 1, interior + 1, axis) - slice_axis(face, 0, interior, axis))

def matmul_batch(left, right):
    return jnp.einsum('fg...,gh...->fh...', left, right, precision=lax.Precision.HIGHEST)

def reference(flow_state, old_state, local_step, azim_flux, axial_flux, block_inverse, lower_block, intersection_first, intersection_weight):
    az_pad = jnp.concatenate([flow_state[..., -2:], flow_state, flow_state[..., :2]], axis=3)
    res_az = jst_residual(az_pad, azim_flux, 3)
    blocks = flow_state.reshape(FIELDS, SPANWISE_TOTAL, N_ROW, AXIAL_DEV, CIRCUMFER_TOTAL)
    upstream = blocks[:, :, :-1, AXIAL_DEV - 2:, :]
    weight = (intersection_weight[1:].astype(jnp.float32) + 0.5) / 8.0
    first = intersection_first[1:].astype(jnp.int32)
    second = (first + 1) % CIRCUMFER_TOTAL
    shape = upstream.shape
    index_one = jnp.broadcast_to(first[None, None, :, None, :], shape)
    index_two = jnp.broadcast_to(second[None, None, :, None, :], shape)
    value_one = jnp.take_along_axis(upstream, index_one, axis=4)
    value_two = jnp.take_along_axis(upstream, index_two, axis=4)
    wide_weight = weight[None, None, :, None, :]
    ghost = wide_weight * value_one + (1.0 - wide_weight) * value_two
    first_row = jnp.broadcast_to(blocks[:, :, 0:1, 0:1, :], (FIELDS, SPANWISE_TOTAL, 1, 2, CIRCUMFER_TOTAL))
    inlet = jnp.concatenate([first_row, ghost], axis=2)
    outlet_ghost = jnp.broadcast_to(blocks[:, :, :, -1:, :], (FIELDS, SPANWISE_TOTAL, N_ROW, 2, CIRCUMFER_TOTAL))
    ax_pad = jnp.concatenate([inlet, blocks, outlet_ghost], axis=3)
    res_ax = jst_residual(ax_pad, axial_flux, 3).reshape(FIELDS, SPANWISE_TOTAL, STREAMWISE_TOTAL, CIRCUMFER_TOTAL)
    residual = res_az + res_ax
    rhs = -local_step[None] * (residual + TIME_FACTOR * (flow_state - old_state))
    coupling = jnp.einsum('fgrxa,ghrxa->fhrxa', block_inverse, lower_block, precision=lax.Precision.HIGHEST)
    source = jnp.einsum('fgrxa,grxa->frxa', block_inverse, rhs, precision=lax.Precision.HIGHEST)
    coup_steps = jnp.moveaxis(coupling, -1, 0)
    source_steps = jnp.moveaxis(source, -1, 0)
    identity = jnp.broadcast_to(jnp.eye(FIELDS, dtype=jnp.float32)[:, :, None, None], (FIELDS, FIELDS, SPANWISE_TOTAL, STREAMWISE_TOTAL))

    def forward(carry, item):
        product, value = carry
        matrix, addend = item
        product = matmul_batch(matrix, product)
        value = jnp.einsum('fg...,g...->f...', matrix, value, precision=lax.Precision.HIGHEST) + addend
        return ((product, value), None)
    start_value = jnp.zeros((FIELDS, SPANWISE_TOTAL, STREAMWISE_TOTAL), jnp.float32)
    (total_prod, total_value), _ = lax.scan(forward, (identity, start_value), (coup_steps, source_steps))
    system = jnp.moveaxis(identity - total_prod, (0, 1), (2, 3))
    target = jnp.moveaxis(total_value, 0, 2)
    closing = jnp.linalg.solve(system, target[..., None])[..., 0]
    closing = jnp.moveaxis(closing, 2, 0)

    def replay(value, item):
        matrix, addend = item
        value = jnp.einsum('fg...,g...->f...', matrix, value, precision=lax.Precision.HIGHEST) + addend
        return (value, value)
    _, sweep = lax.scan(replay, closing, (coup_steps, source_steps))
    update = jnp.moveaxis(sweep, 0, -1)
    return flow_state + update
```

```python
import functools

import jax
import jax.numpy as jnp
from jax import lax
from jax.experimental import pallas as pl
from jax.experimental.pallas import tpu as pltpu
from jax.sharding import PartitionSpec as P

FIELDS = 6
LANES = 128
HALF = 8
HALO = 72
JST_SECOND = 0.5
JST_FOURTH = 1.0 / 32.0
TIME_FACTOR = 1.5
VMEM = pl.BlockSpec(memory_space=pltpu.VMEM)
HBM = pl.BlockSpec(memory_space=pltpu.HBM)


def lane_ids():
    return lax.broadcasted_iota(jnp.int32, (HALF, LANES), 1)


def roll_lanes(x, shift):
    shift = shift % LANES
    return x if isinstance(shift, int) and shift == 0 else pltpu.roll(x, shift, 1)


def rows(half):
    return pl.ds(half * HALF, HALF)


def packing(sectors):
    return LANES // (2 * sectors)


def product(left, right):
    out = []
    for f in range(FIELDS):
        for h in range(FIELDS):
            acc = left[f * FIELDS] * right[h]
            for g in range(1, FIELDS):
                acc = acc + left[f * FIELDS + g] * right[g * FIELDS + h]
            out.append(acc)
    return out


def matvec(matrix, vector):
    out = []
    for f in range(FIELDS):
        acc = matrix[f * FIELDS] * vector[0]
        for g in range(1, FIELDS):
            acc = acc + matrix[f * FIELDS + g] * vector[g]
        out.append(acc)
    return out


def pack_last_lane(values, lane, base, width):
    acc = jnp.zeros((HALF, LANES), jnp.float32)
    for entry, pair in enumerate(values):
        for half in range(2):
            target = base + width * entry + half
            acc = jnp.where(lane == target, roll_lanes(pair[half], target + 1), acc)
    return acc


def routes(sectors, place, cell):
    turn = (cell // LANES - place) & (sectors - 1)
    flags = []
    for bit in reversed(range(sectors.bit_length() - 1)):
        low = place & ((1 << bit) - 1)
        for k in (turn, (turn + 1) & (sectors - 1)):
            borrow = jnp.where(low < (k & ((1 << bit) - 1)), 1, 0)
            flags.append(((k >> bit) & 1) ^ borrow)
    return flags


def prepare_kernel(
    sectors,
    levels,
    flow_in,
    old_in,
    step_in,
    azf_in,
    axf_in,
    inverse_in,
    lower_in,
    first_in,
    weight_in,
    flow,
    gain,
    source,
    coef,
    flags,
    packed,
    scan,
    old,
    step_size,
    azf,
    axf,
    inverse,
    lower,
    first,
    weight,
    sems,
):
    copies = [
        pltpu.make_async_copy(src, dst, sems.at[at])
        for at, (src, dst) in enumerate(
            (
                (inverse_in, inverse),
                (lower_in, lower),
                (flow_in, flow),
                (old_in, old),
                (step_in, step_size),
                (azf_in, azf),
                (axf_in, axf),
                (first_in, first),
                (weight_in, weight),
            )
        )
    ]
    for copy in copies:
        copy.start()
    lane = lane_ids()
    place = lax.axis_index("azim")
    for copy in copies:
        copy.wait()
    row = lax.broadcasted_iota(jnp.int32, (1, LANES), 1) * 0
    cell = row + jnp.broadcast_to(first[:, 0:1], (1, LANES))
    for at, flag in enumerate(routes(sectors, row + place, cell)):
        flags[pl.ds(at, 1), :] = flag
    flags[pl.ds(flags.shape[0] - 1, 1), :] = cell & (LANES - 1)
    for f in range(FIELDS):
        for g in range(FIELDS):
            at = f * FIELDS + g
            coef[pl.ds(at, 1), :] = jnp.broadcast_to(azf[f : f + 1, g : g + 1], (1, LANES))
            coef[pl.ds(36 + at, 1), :] = jnp.broadcast_to(axf[f : f + 1, g : g + 1], (1, LANES))
    coef[pl.ds(72, 1), :] = (weight[...].astype(jnp.float32) + 0.5) / 8.0
    for half in range(2):
        left = [inverse[e, rows(half), :] for e in range(36)]
        right = [lower[e, rows(half), :] for e in range(36)]
        for e, value in enumerate(product(left, right)):
            scan[e, rows(half), :] = value
    for half in range(2):
        minus_step = -step_size[rows(half), :]
        scaled = [minus_step * inverse[e, rows(half), :] for e in range(36)]
        change = [TIME_FACTOR * (flow[f, rows(half), :] - old[f, rows(half), :]) for f in range(FIELDS)]
        for e in range(36):
            gain[e, rows(half), :] = scaled[e]
        for f, value in enumerate(matvec(scaled, change)):
            source[f, rows(half), :] = value
    for level in range(levels):
        step = 1 << level
        keep = lane < step
        for half in range(2):
            later = [scan[36 * level + e, rows(half), :] for e in range(36)]
            earlier = [roll_lanes(x, step) for x in later]
            for e, value in enumerate(product(later, earlier)):
                scan[36 * (level + 1) + e, rows(half), :] = jnp.where(keep, later[e], value)
    acc = pack_last_lane(
        [[scan[36 * levels + e, rows(half), :] for half in range(2)] for e in range(36)], lane, 0, 2
    )
    for f in range(FIELDS):
        for half in range(2):
            start = HALO + 4 * (2 * f + half)
            u = flow[f, rows(half), :]
            acc = jnp.where((lane >= start) & (lane < start + 2), roll_lanes(u, start), acc)
            acc = jnp.where((lane >= start + 2) & (lane < start + 4), roll_lanes(u, start + 4), acc)
    packed[...] = acc


def jst_parts(u0, um1, um2, up1, up2):
    p0, pm1, pm2, pp1, pp2 = [1.0 + x[0] * x[0] for x in (u0, um1, um2, up1, up2)]

    def sensor(up, mid, down):
        return jnp.abs(up - 2.0 * mid + down) / (up + 2.0 * mid + down)

    mid = sensor(pp1, p0, pm1)
    e2r = JST_SECOND * jnp.maximum(mid, sensor(pp2, pp1, p0))
    e2l = JST_SECOND * jnp.maximum(sensor(p0, pm1, pm2), mid)
    e4r = jnp.maximum(0.0, JST_FOURTH - e2r)
    e4l = jnp.maximum(0.0, JST_FOURTH - e2l)
    central, faces = [], []
    for f in range(FIELDS):
        dr = up1[f] - u0[f]
        dl = u0[f] - um1[f]
        third_r = up2[f] - 3.0 * up1[f] + 3.0 * u0[f] - um1[f]
        third_l = up1[f] - 3.0 * u0[f] + 3.0 * um1[f] - um2[f]
        central.append(0.5 * (up1[f] - um1[f]))
        faces.append((e2r * dr - e4r * third_r) - (e2l * dl - e4l * third_l))
    return central, faces


def position(sectors, difference):
    bits = sectors.bit_length() - 1
    at = 0
    for bit in range(bits):
        at = at + (((difference >> bit) & 1) << (bits - 1 - bit))
    return at


def source_kernel(
    sectors, levels, ring_a, ring_b, ring, flow, gain, source, coef, flags, scan, sweep, packed
):
    lane = lane_ids()
    sub = lax.broadcasted_iota(jnp.int32, (HALF, LANES), 0)
    place = lax.axis_index("azim")
    row = lax.axis_index("row")
    left_pack = ring[position(sectors, place ^ ((place + sectors - 1) & (sectors - 1)))]
    right_pack = ring[position(sectors, place ^ ((place + 1) & (sectors - 1)))]
    shift = flags[flags.shape[0] - 1, 0]
    back = (LANES - shift) & (LANES - 1)

    def coefficient(at):
        return jnp.broadcast_to(coef[pl.ds(at, 1), :], (HALF, LANES))

    frac = coefficient(72)
    ghost = []
    for f in range(FIELDS):
        a = pltpu.roll(ring_a[pl.ds(f * HALF, HALF), :], back, 1)
        b = pltpu.roll(ring_b[pl.ds(f * HALF, HALF), :], back, 1)
        one = jnp.where(lane < LANES - shift, a, b)
        two = pltpu.roll(jnp.where(lane == 0, b, one), LANES - 1, 1)
        ghost.append(frac * one + (1.0 - frac) * two)
    halo = jnp.where((lane & 3) < 2, right_pack, left_pack)
    axial = sub % 4
    is_first_row = row == 0
    for half in range(2):
        u0 = [flow[f, rows(half), :] for f in range(FIELDS)]
        um1, um2, up1, up2 = [], [], [], []
        for f in range(FIELDS):
            start = HALO + 4 * (2 * f + half)
            edge = roll_lanes(halo, LANES - 2 - start)
            um1.append(jnp.where(lane < 1, roll_lanes(halo, -(start + 3)), roll_lanes(u0[f], 1)))
            um2.append(jnp.where(lane < 2, edge, roll_lanes(u0[f], 2)))
            up1.append(jnp.where(lane >= LANES - 1, roll_lanes(halo, LANES - 1 - start), roll_lanes(u0[f], -1)))
            up2.append(jnp.where(lane >= LANES - 2, edge, roll_lanes(u0[f], -2)))
        az_central, az_faces = jst_parts(u0, um1, um2, up1, up2)
        um1, um2, up1, up2 = [], [], [], []
        for f in range(FIELDS):
            g = ghost[f]
            if half == 0:
                spread = jnp.where(sub < 4, g, pltpu.roll(g, 2, 0))
            else:
                spread = jnp.where(sub < 4, pltpu.roll(g, 4, 0), pltpu.roll(g, 6, 0))
            u = u0[f]
            down1 = pltpu.roll(u, 1, 0)
            down2 = pltpu.roll(u, 2, 0)
            lift1 = pltpu.roll(u, HALF - 1, 0)
            lift2 = pltpu.roll(u, HALF - 2, 0)
            same = jnp.where(axial == 0, u, down1)
            spread = jnp.where(is_first_row, same, spread)
            next_ghost = pltpu.roll(spread, HALF - 1, 0)
            um1.append(jnp.where(axial == 0, next_ghost, down1))
            um2.append(jnp.where(axial < 2, spread, down2))
            last1 = jnp.where(axial == 3, u, lift1)
            up1.append(last1)
            up2.append(jnp.where(axial == 3, u, jnp.where(axial == 2, lift1, lift2)))
        ax_central, ax_faces = jst_parts(u0, um1, um2, up1, up2)
        residual = []
        for f in range(FIELDS):
            acc = -(az_faces[f] + ax_faces[f])
            for g in range(FIELDS):
                at = f * FIELDS + g
                acc = acc + coefficient(at) * az_central[g] + coefficient(36 + at) * ax_central[g]
            residual.append(acc)
        added = matvec([gain[e, rows(half), :] for e in range(36)], residual)
        for f in range(FIELDS):
            sweep[f, rows(half), :] = source[f, rows(half), :] + added[f]
    values = [[sweep[f, rows(half), :] for half in range(2)] for f in range(FIELDS)]
    for level in range(levels):
        step = 1 << level
        for half in range(2):
            before = [jnp.where(lane < step, 0.0, roll_lanes(values[f][half], step)) for f in range(FIELDS)]
            matrix = [scan[36 * level + e, rows(half), :] for e in range(36)]
            for f, gain in enumerate(matvec(matrix, before)):
                values[f][half] = values[f][half] + gain
    for f in range(FIELDS):
        for half in range(2):
            sweep[f, rows(half), :] = values[f][half]
    per = packing(sectors)
    for at in range(0, FIELDS, per):
        value = pack_last_lane(values[at : at + per], lane, 0, 2 * sectors)
        packed[pl.ds(HALF * (at // per), HALF), :] = roll_lanes(value, 2 * place)


def relative(pack, entry, sectors, place, lane):
    per = packing(sectors)
    width = 2 * sectors
    base = (entry % per) * width
    row = pack[pl.ds(HALF * (entry // per), HALF), :]
    turn = 2 * place
    here = pltpu.roll(row, lax.rem(2 * LANES - base - turn, LANES), 1)
    wrapped = pltpu.roll(row, lax.rem(2 * LANES - base - turn + width, LANES), 1)
    return jnp.where(lane < width - turn, here, wrapped)


def closing_kernel(sectors, ring, suffix, closing):
    lane = lane_ids()
    place = lax.axis_index("azim")
    width = 2 * sectors
    one = [jnp.float32(1.0 if e % 7 == 0 else 0.0) for e in range(36)]
    turned = []
    for t in range(sectors):
        at = position(sectors, place ^ ((place + t) & (sectors - 1)))
        turned.append(roll_lanes(ring[at], 2 * t))
    pair = lane >> 1
    maps = []
    for e in range(36):
        acc = turned[0]
        for t in range(1, sectors):
            acc = jnp.where(pair == (e + t) % (LANES // 2), turned[t], acc)
        maps.append(roll_lanes(acc, -2 * e))
    step = 2
    while step < width:
        later = [jnp.where(lane < width - step, roll_lanes(x, -step), one[e]) for e, x in enumerate(maps)]
        maps = product(later, maps)
        step *= 2
    for e in range(36):
        suffix[e] = jnp.where(lane < width - 2, roll_lanes(maps[e], -2), one[e])
    system = [[one[f * 6 + g] - maps[f * 6 + g] for g in range(6)] for f in range(6)]
    result = [[jnp.full((HALF, LANES), one[f * 6 + g]) for g in range(6)] for f in range(6)]
    for pivot in range(6):
        scale = 1.0 / system[pivot][pivot]
        for g in range(pivot + 1, 6):
            system[pivot][g] = system[pivot][g] * scale
        for g in range(pivot + 1):
            result[pivot][g] = result[pivot][g] * scale
        for f in range(6):
            if f == pivot:
                continue
            factor = system[f][pivot]
            for g in range(pivot + 1, 6):
                system[f][g] = system[f][g] - factor * system[pivot][g]
            for g in range(pivot + 1):
                result[f][g] = result[f][g] - factor * result[pivot][g]
    for f in range(6):
        for g in range(6):
            closing[f * 6 + g] = result[f][g]


def finish_kernel(sectors, levels, gathered, suffix, closing, flow, scan, sweep, out):
    lane = lane_ids()
    place = lax.axis_index("azim")
    width = 2 * sectors
    ends = [relative(gathered, f, sectors, place, lane) for f in range(FIELDS)]
    total = matvec([suffix[e] for e in range(36)], ends)
    step = width // 2
    while step >= 2:
        total = [x + roll_lanes(x, -step) for x in total]
        step //= 2
    start = matvec([closing[e] for e in range(36)], total)
    for half in range(2):
        begin = [jnp.broadcast_to(x[:, half : half + 1], (HALF, LANES)) for x in start]
        gain = matvec([scan[e, rows(half), :] for e in range(36)], begin)
        for f in range(FIELDS):
            out[f, rows(half), :] = flow[f, rows(half), :] + (gain[f] + sweep[f, rows(half), :])


def shape(*dims):
    return jax.ShapeDtypeStruct(dims, jnp.float32)


def shards(
    sectors,
    row_count,
    flow_state,
    old_state,
    local_step,
    azim_flux,
    axial_flux,
    block_inverse,
    lower_block,
    intersection_first,
    intersection_weight,
):
    radial, axial, cells = flow_state.shape[1:]
    lines = radial * axial
    levels = cells.bit_length() - 1
    end_rows = HALF * pl.cdiv(FIELDS, packing(sectors))
    flag_rows = HALF * pl.cdiv(2 * sectors.bit_length() - 1, HALF)
    call = functools.partial(
        pl.pallas_call, compiler_params=pltpu.CompilerParams(vmem_limit_bytes=16 << 20)
    )

    upstream = lax.ppermute(flow_state, "row", [(r, (r + 1) % row_count) for r in range(row_count)])
    flow, gain, source, coef, flags, ring, scan = call(
        functools.partial(prepare_kernel, sectors, levels),
        out_shape=(
            shape(FIELDS, lines, cells),
            shape(36, lines, cells),
            shape(FIELDS, lines, cells),
            shape(80, cells),
            jax.ShapeDtypeStruct((flag_rows, cells), jnp.int32),
            shape(HALF, cells),
            shape(36 * (levels + 1), lines, cells),
        ),
        in_specs=[HBM] * 9,
        out_specs=(VMEM,) * 7,
        scratch_shapes=[
            pltpu.VMEM((FIELDS, lines, cells), jnp.float32),
            pltpu.VMEM((lines, cells), jnp.float32),
            pltpu.VMEM((FIELDS, FIELDS), jnp.float32),
            pltpu.VMEM((FIELDS, FIELDS), jnp.float32),
            pltpu.VMEM((36, lines, cells), jnp.float32),
            pltpu.VMEM((36, lines, cells), jnp.float32),
            pltpu.VMEM((1, cells), jnp.int32),
            pltpu.VMEM((1, cells), jnp.int32),
            pltpu.SemaphoreType.DMA((9,)),
        ],
    )(
        *(
            pltpu.with_memory_space_constraint(x, pltpu.HBM)
            for x in (
                flow_state.reshape(FIELDS, lines, cells),
                old_state.reshape(FIELDS, lines, cells),
                local_step.reshape(lines, cells),
                azim_flux,
                axial_flux,
                block_inverse.reshape(36, lines, cells),
                lower_block.reshape(36, lines, cells),
                intersection_first,
                intersection_weight,
            )
        )
    )
    ring_a = ring_b = upstream[:, :, axial - 2 :, :].reshape(FIELDS * HALF, cells)
    at, mask = 0, sectors // 2
    while mask:
        from_a = flags[at : at + 1] != 0
        from_b = flags[at + 1 : at + 2] != 0
        sent = jnp.concatenate([jnp.where(from_a, ring_a, ring_b), ring], axis=0)
        arrived = lax.ppermute(sent, "azim", [(i, i ^ mask) for i in range(sectors)])
        upper = arrived[: FIELDS * HALF]
        ring_a = jnp.where(from_a, upper, ring_a)
        ring_b = jnp.where(from_b, upper, ring_b)
        ring = jnp.concatenate([ring, arrived[FIELDS * HALF :]], axis=0)
        at, mask = at + 2, mask // 2
    ring = ring.reshape(sectors, HALF, cells)

    sweep, ends = call(
        functools.partial(source_kernel, sectors, levels),
        out_shape=(shape(FIELDS, lines, cells), shape(end_rows, cells)),
        in_specs=[VMEM] * 9,
        out_specs=(VMEM, VMEM),
    )(ring_a, ring_b, ring, flow, gain, source, coef, flags, scan)
    suffix, closing = call(
        functools.partial(closing_kernel, sectors),
        out_shape=(shape(36, HALF, LANES), shape(36, HALF, LANES)),
        in_specs=[VMEM],
        out_specs=(VMEM, VMEM),
    )(ring)
    mask = 1
    while mask < sectors:
        ends = ends + lax.ppermute(ends, "azim", [(i, i ^ mask) for i in range(sectors)])
        mask *= 2
    new_state = call(
        functools.partial(finish_kernel, sectors, levels),
        out_shape=shape(FIELDS, lines, cells),
        in_specs=[VMEM] * 6,
        out_specs=VMEM,
    )(ends, suffix, closing, flow, scan[36 * levels :], sweep)
    return new_state.reshape(flow_state.shape)


def solution(mesh):
    return jax.shard_map(
        functools.partial(shards, mesh.shape["azim"], mesh.shape["row"]),
        mesh=mesh,
        in_specs=(
            P(None, None, "row", "azim"),
            P(None, None, "row", "azim"),
            P(None, "row", "azim"),
            P(),
            P(),
            P(None, None, None, "row", "azim"),
            P(None, None, None, "row", "azim"),
            P("row", "azim"),
            P("row", "azim"),
        ),
        out_specs=P(None, None, "row", "azim"),
        check_vma=False,
    )
```

```python
import functools

import jax
import jax.numpy as jnp
from jax import lax
from jax.experimental import pallas as pl
from jax.experimental.pallas import tpu as pltpu
from jax.sharding import PartitionSpec as P

FIELDS = 6
LANES = 128
HALF = 8
HALO = 72
JST_SECOND = 0.5
JST_FOURTH = 1.0 / 32.0
TIME_FACTOR = 1.5
VMEM = pl.BlockSpec(memory_space=pltpu.VMEM)
HBM = pl.BlockSpec(memory_space=pltpu.HBM)


def lane_ids():
    return lax.broadcasted_iota(jnp.int32, (HALF, LANES), 1)


def roll_lanes(x, shift):
    shift = shift % LANES
    return x if isinstance(shift, int) and shift == 0 else pltpu.roll(x, shift, 1)


def rows(half):
    return pl.ds(half * HALF, HALF)


def packing(sectors):
    return LANES // (2 * sectors)


def product(left, right):
    out = []
    for f in range(FIELDS):
        for h in range(FIELDS):
            acc = left[f * FIELDS] * right[h]
            for g in range(1, FIELDS):
                acc = acc + left[f * FIELDS + g] * right[g * FIELDS + h]
            out.append(acc)
    return out


def matvec(matrix, vector):
    out = []
    for f in range(FIELDS):
        acc = matrix[f * FIELDS] * vector[0]
        for g in range(1, FIELDS):
            acc = acc + matrix[f * FIELDS + g] * vector[g]
        out.append(acc)
    return out


def pack_last_lane(values, lane, base, width):
    acc = jnp.zeros((HALF, LANES), jnp.float32)
    for entry, pair in enumerate(values):
        for half in range(2):
            target = base + width * entry + half
            acc = jnp.where(lane == target, roll_lanes(pair[half], target + 1), acc)
    return acc


def groups(sectors):
    bits = sectors.bit_length() - 1
    found = []
    for low in reversed(range(0, bits - 1, 2)):
        found.append((1 << low, 2 << low, 3 << low))
    return found


def routes(sectors, place, cell):
    turn = (cell // LANES - place) & (sectors - 1)
    turns = (turn, (turn + 1) & (sectors - 1))
    flags = []
    half = sectors // 2
    for k in turns:
        borrow = jnp.where((place & (half - 1)) < (k & (half - 1)), half, 0)
        flags.append((k & half) ^ borrow)
    for unit, _, _ in groups(sectors):
        span = 4 * unit - 1
        mine = place & span & -unit
        for k in turns:
            low = (place - k) & (unit - 1)
            flags.append(mine ^ ((mine + low + k) & span & -unit))
        flags.append(mine ^ ((place - turn) & span & -unit))
    return flags


def edges_kernel(flow_in, flow, outlet, halo, sem):
    copy = pltpu.make_async_copy(flow_in, flow, sem)
    copy.start()
    lane = lane_ids()
    sub = lax.broadcasted_iota(jnp.int32, (HALF, LANES), 0)
    copy.wait()
    acc = jnp.zeros((HALF, LANES), jnp.float32)
    for f in range(FIELDS):
        lower, upper = flow[f, rows(0), :], flow[f, rows(1), :]
        outlet[pl.ds(f * HALF, HALF), :] = jnp.where((sub & 3) >= 2, lower, pltpu.roll(upper, HALF - 2, 0))
        for half, u in enumerate((lower, upper)):
            start = HALO + 4 * (2 * f + half)
            acc = jnp.where((lane >= start) & (lane < start + 2), roll_lanes(u, start), acc)
            acc = jnp.where((lane >= start + 2) & (lane < start + 4), roll_lanes(u, start + 4), acc)
    halo[...] = acc


def prepare_kernel(
    sectors,
    levels,
    flow,
    halo,
    old_in,
    step_in,
    azf_in,
    axf_in,
    inverse_in,
    lower_in,
    first_in,
    weight_in,
    gain,
    source,
    coef,
    flags,
    packed,
    scan,
    old,
    step_size,
    azf,
    axf,
    inverse,
    lower,
    first,
    weight,
    sems,
):
    copies = [
        pltpu.make_async_copy(src, dst, sems.at[at])
        for at, (src, dst) in enumerate(
            (
                (inverse_in, inverse),
                (lower_in, lower),
                (old_in, old),
                (step_in, step_size),
                (azf_in, azf),
                (axf_in, axf),
                (first_in, first),
                (weight_in, weight),
            )
        )
    ]
    for copy in copies:
        copy.start()
    lane = lane_ids()
    place = lax.axis_index("azim")
    for copy in copies:
        copy.wait()
    row = lax.broadcasted_iota(jnp.int32, (1, LANES), 1) * 0
    cell = row + jnp.broadcast_to(first[:, 0:1], (1, LANES))
    for at, flag in enumerate(routes(sectors, row + place, cell)):
        flags[pl.ds(at, 1), :] = flag
    flags[pl.ds(flags.shape[0] - 1, 1), :] = cell & (LANES - 1)
    for f in range(FIELDS):
        for g in range(FIELDS):
            at = f * FIELDS + g
            coef[pl.ds(at, 1), :] = jnp.broadcast_to(azf[f : f + 1, g : g + 1], (1, LANES))
            coef[pl.ds(36 + at, 1), :] = jnp.broadcast_to(axf[f : f + 1, g : g + 1], (1, LANES))
    coef[pl.ds(72, 1), :] = (weight[...].astype(jnp.float32) + 0.5) / 8.0
    for half in range(2):
        left = [inverse[e, rows(half), :] for e in range(36)]
        right = [lower[e, rows(half), :] for e in range(36)]
        for e, value in enumerate(product(left, right)):
            scan[e, rows(half), :] = value
    for half in range(2):
        minus_step = -step_size[rows(half), :]
        scaled = [minus_step * inverse[e, rows(half), :] for e in range(36)]
        change = [TIME_FACTOR * (flow[f, rows(half), :] - old[f, rows(half), :]) for f in range(FIELDS)]
        for e in range(36):
            gain[e, rows(half), :] = scaled[e]
        for f, value in enumerate(matvec(scaled, change)):
            source[f, rows(half), :] = value
    for level in range(levels):
        step = 1 << level
        keep = lane < step
        for half in range(2):
            later = [scan[36 * level + e, rows(half), :] for e in range(36)]
            earlier = [roll_lanes(x, step) for x in later]
            for e, value in enumerate(product(later, earlier)):
                scan[36 * (level + 1) + e, rows(half), :] = jnp.where(keep, later[e], value)
    acc = pack_last_lane(
        [[scan[36 * levels + e, rows(half), :] for half in range(2)] for e in range(36)], lane, 0, 2
    )
    packed[...] = jnp.where(lane < HALO, acc, halo[...])


def jst_parts(u0, um1, um2, up1, up2):
    p0, pm1, pm2, pp1, pp2 = [1.0 + x[0] * x[0] for x in (u0, um1, um2, up1, up2)]

    def sensor(up, mid, down):
        return jnp.abs(up - 2.0 * mid + down) / (up + 2.0 * mid + down)

    mid = sensor(pp1, p0, pm1)
    e2r = JST_SECOND * jnp.maximum(mid, sensor(pp2, pp1, p0))
    e2l = JST_SECOND * jnp.maximum(sensor(p0, pm1, pm2), mid)
    e4r = jnp.maximum(0.0, JST_FOURTH - e2r)
    e4l = jnp.maximum(0.0, JST_FOURTH - e2l)
    central, faces = [], []
    for f in range(FIELDS):
        dr = up1[f] - u0[f]
        dl = u0[f] - um1[f]
        third_r = up2[f] - 3.0 * up1[f] + 3.0 * u0[f] - um1[f]
        third_l = up1[f] - 3.0 * u0[f] + 3.0 * um1[f] - um2[f]
        central.append(0.5 * (up1[f] - um1[f]))
        faces.append((e2r * dr - e4r * third_r) - (e2l * dl - e4l * third_l))
    return central, faces


def gathered_at(sectors, difference):
    at, count = 0, 1
    for unit, _, _ in groups(sectors):
        at = at + ((difference // unit) & 3) * count
        count *= 4
    return at


def halo_at(sectors, difference):
    return 2 * gathered_at(sectors, difference) + difference // (sectors // 2)


def map_at(sectors, difference):
    return gathered_at(sectors, difference) + (difference // (sectors // 2)) * (sectors // 2)


def source_kernel(
    sectors, levels, ring_a, ring_b, ring, flow, gain, source, coef, flags, scan, sweep, packed
):
    lane = lane_ids()
    sub = lax.broadcasted_iota(jnp.int32, (HALF, LANES), 0)
    place = lax.axis_index("azim")
    row = lax.axis_index("row")
    left_pack = ring[halo_at(sectors, place ^ ((place + sectors - 1) & (sectors - 1)))]
    right_pack = ring[halo_at(sectors, place ^ ((place + 1) & (sectors - 1)))]
    shift = flags[flags.shape[0] - 1, 0]
    back = (LANES - shift) & (LANES - 1)

    def coefficient(at):
        return jnp.broadcast_to(coef[pl.ds(at, 1), :], (HALF, LANES))

    frac = coefficient(72)
    ghost = []
    for f in range(FIELDS):
        a = pltpu.roll(ring_a[pl.ds(f * HALF, HALF), :], back, 1)
        b = pltpu.roll(ring_b[pl.ds(f * HALF, HALF), :], back, 1)
        one = jnp.where(lane < LANES - shift, a, b)
        two = pltpu.roll(jnp.where(lane == 0, b, one), LANES - 1, 1)
        ghost.append(frac * one + (1.0 - frac) * two)
    halo = jnp.where((lane & 3) < 2, right_pack, left_pack)
    axial = sub % 4
    is_first_row = row == 0
    for half in range(2):
        u0 = [flow[f, rows(half), :] for f in range(FIELDS)]
        um1, um2, up1, up2 = [], [], [], []
        for f in range(FIELDS):
            start = HALO + 4 * (2 * f + half)
            edge = roll_lanes(halo, LANES - 2 - start)
            um1.append(jnp.where(lane < 1, roll_lanes(halo, -(start + 3)), roll_lanes(u0[f], 1)))
            um2.append(jnp.where(lane < 2, edge, roll_lanes(u0[f], 2)))
            up1.append(jnp.where(lane >= LANES - 1, roll_lanes(halo, LANES - 1 - start), roll_lanes(u0[f], -1)))
            up2.append(jnp.where(lane >= LANES - 2, edge, roll_lanes(u0[f], -2)))
        az_central, az_faces = jst_parts(u0, um1, um2, up1, up2)
        um1, um2, up1, up2 = [], [], [], []
        for f in range(FIELDS):
            g = ghost[f]
            spread = pltpu.roll(g, HALF - 2, 0) if half == 0 else g
            u = u0[f]
            down1 = pltpu.roll(u, 1, 0)
            down2 = pltpu.roll(u, 2, 0)
            lift1 = pltpu.roll(u, HALF - 1, 0)
            lift2 = pltpu.roll(u, HALF - 2, 0)
            same = jnp.where(axial == 0, u, down1)
            spread = jnp.where(is_first_row, same, spread)
            next_ghost = pltpu.roll(spread, HALF - 1, 0)
            um1.append(jnp.where(axial == 0, next_ghost, down1))
            um2.append(jnp.where(axial < 2, spread, down2))
            last1 = jnp.where(axial == 3, u, lift1)
            up1.append(last1)
            up2.append(jnp.where(axial == 3, u, jnp.where(axial == 2, lift1, lift2)))
        ax_central, ax_faces = jst_parts(u0, um1, um2, up1, up2)
        residual = []
        for f in range(FIELDS):
            acc = -(az_faces[f] + ax_faces[f])
            for g in range(FIELDS):
                at = f * FIELDS + g
                acc = acc + coefficient(at) * az_central[g] + coefficient(36 + at) * ax_central[g]
            residual.append(acc)
        added = matvec([gain[e, rows(half), :] for e in range(36)], residual)
        for f in range(FIELDS):
            sweep[f, rows(half), :] = source[f, rows(half), :] + added[f]
    values = [[sweep[f, rows(half), :] for half in range(2)] for f in range(FIELDS)]
    for level in range(levels):
        step = 1 << level
        for half in range(2):
            before = [jnp.where(lane < step, 0.0, roll_lanes(values[f][half], step)) for f in range(FIELDS)]
            matrix = [scan[36 * level + e, rows(half), :] for e in range(36)]
            for f, gain in enumerate(matvec(matrix, before)):
                values[f][half] = values[f][half] + gain
    for f in range(FIELDS):
        for half in range(2):
            sweep[f, rows(half), :] = values[f][half]
    per = packing(sectors)
    for at in range(0, FIELDS, per):
        value = pack_last_lane(values[at : at + per], lane, 0, 2 * sectors)
        packed[pl.ds(HALF * (at // per), HALF), :] = roll_lanes(value, 2 * place)


def relative(pack, entry, sectors, place, lane):
    per = packing(sectors)
    width = 2 * sectors
    base = (entry % per) * width
    row = pack[pl.ds(HALF * (entry // per), HALF), :]
    turn = 2 * place
    here = pltpu.roll(row, lax.rem(2 * LANES - base - turn, LANES), 1)
    wrapped = pltpu.roll(row, lax.rem(2 * LANES - base - turn + width, LANES), 1)
    return jnp.where(lane < width - turn, here, wrapped)


def closing_kernel(sectors, ring, suffix, closing):
    lane = lane_ids()
    place = lax.axis_index("azim")
    width = 2 * sectors
    one = [jnp.float32(1.0 if e % 7 == 0 else 0.0) for e in range(36)]
    turned = []
    for t in range(sectors):
        at = map_at(sectors, place ^ ((place + t) & (sectors - 1)))
        turned.append(roll_lanes(ring[at], 2 * t))
    pair = lane >> 1
    maps = []
    for e in range(36):
        acc = turned[0]
        for t in range(1, sectors):
            acc = jnp.where(pair == (e + t) % (LANES // 2), turned[t], acc)
        maps.append(roll_lanes(acc, -2 * e))
    step = 2
    while step < width:
        later = [jnp.where(lane < width - step, roll_lanes(x, -step), one[e]) for e, x in enumerate(maps)]
        maps = product(later, maps)
        step *= 2
    for e in range(36):
        suffix[e] = jnp.where(lane < width - 2, roll_lanes(maps[e], -2), one[e])
    system = [[one[f * 6 + g] - maps[f * 6 + g] for g in range(6)] for f in range(6)]
    result = [[jnp.full((HALF, LANES), one[f * 6 + g]) for g in range(6)] for f in range(6)]
    for pivot in range(6):
        scale = 1.0 / system[pivot][pivot]
        for g in range(pivot + 1, 6):
            system[pivot][g] = system[pivot][g] * scale
        for g in range(pivot + 1):
            result[pivot][g] = result[pivot][g] * scale
        for f in range(6):
            if f == pivot:
                continue
            factor = system[f][pivot]
            for g in range(pivot + 1, 6):
                system[f][g] = system[f][g] - factor * system[pivot][g]
            for g in range(pivot + 1):
                result[f][g] = result[f][g] - factor * result[pivot][g]
    for f in range(6):
        for g in range(6):
            closing[f * 6 + g] = result[f][g]


def finish_kernel(sectors, levels, gathered, suffix, closing, flow, scan, sweep, out):
    lane = lane_ids()
    place = lax.axis_index("azim")
    width = 2 * sectors
    ends = [relative(gathered, f, sectors, place, lane) for f in range(FIELDS)]
    total = matvec([suffix[e] for e in range(36)], ends)
    step = width // 2
    while step >= 2:
        total = [x + roll_lanes(x, -step) for x in total]
        step //= 2
    start = matvec([closing[e] for e in range(36)], total)
    for half in range(2):
        begin = [jnp.broadcast_to(x[:, half : half + 1], (HALF, LANES)) for x in start]
        gain = matvec([scan[36 * levels + e, rows(half), :] for e in range(36)], begin)
        for f in range(FIELDS):
            out[f, rows(half), :] = flow[f, rows(half), :] + (gain[f] + sweep[f, rows(half), :])


def exchange(values, sectors, mask):
    return lax.ppermute(values, "azim", [(i, i ^ mask) for i in range(sectors)])


def from_upstream(values, sectors, row_count, mask):
    return lax.ppermute(
        values,
        ("azim", "row"),
        [
            (i * row_count + r, (i ^ mask) * row_count + (r + 1) % row_count)
            for i in range(sectors)
            for r in range(row_count)
        ],
    )


def in_hbm(x):
    return pltpu.with_memory_space_constraint(x, pltpu.HBM)


def shape(*dims):
    return jax.ShapeDtypeStruct(dims, jnp.float32)


def shards(
    sectors,
    row_count,
    flow_state,
    old_state,
    local_step,
    azim_flux,
    axial_flux,
    block_inverse,
    lower_block,
    intersection_first,
    intersection_weight,
):
    radial, axial, cells = flow_state.shape[1:]
    lines = radial * axial
    levels = cells.bit_length() - 1
    end_rows = HALF * pl.cdiv(FIELDS, packing(sectors))
    flag_rows = HALF * pl.cdiv(3 * sectors.bit_length(), HALF)
    count = FIELDS * HALF
    call = functools.partial(
        pl.pallas_call, compiler_params=pltpu.CompilerParams(vmem_limit_bytes=16 << 20)
    )

    flow, outlet, halo = call(
        edges_kernel,
        out_shape=(shape(FIELDS, lines, cells), shape(count, cells), shape(HALF, cells)),
        in_specs=[HBM],
        out_specs=(VMEM,) * 3,
        scratch_shapes=[pltpu.SemaphoreType.DMA(())],
    )(in_hbm(flow_state.reshape(FIELDS, lines, cells)))
    top = sectors // 2
    upstream_far = from_upstream(outlet, sectors, row_count, top)
    halo_far = exchange(halo, sectors, top)
    upstream = from_upstream(outlet, sectors, row_count, 0)
    gain, source, coef, flags, packed, scan = call(
        functools.partial(prepare_kernel, sectors, levels),
        out_shape=(
            shape(36, lines, cells),
            shape(FIELDS, lines, cells),
            shape(80, cells),
            jax.ShapeDtypeStruct((flag_rows, cells), jnp.int32),
            shape(HALF, cells),
            shape(36 * (levels + 1), lines, cells),
        ),
        in_specs=[VMEM] * 2 + [HBM] * 8,
        out_specs=(VMEM,) * 6,
        scratch_shapes=[
            pltpu.VMEM((FIELDS, lines, cells), jnp.float32),
            pltpu.VMEM((lines, cells), jnp.float32),
            pltpu.VMEM((FIELDS, FIELDS), jnp.float32),
            pltpu.VMEM((FIELDS, FIELDS), jnp.float32),
            pltpu.VMEM((36, lines, cells), jnp.float32),
            pltpu.VMEM((36, lines, cells), jnp.float32),
            pltpu.VMEM((1, cells), jnp.int32),
            pltpu.VMEM((1, cells), jnp.int32),
            pltpu.SemaphoreType.DMA((8,)),
        ],
    )(
        flow,
        halo,
        *(
            in_hbm(x)
            for x in (
                old_state.reshape(FIELDS, lines, cells),
                local_step.reshape(lines, cells),
                azim_flux,
                axial_flux,
                block_inverse.reshape(36, lines, cells),
                lower_block.reshape(36, lines, cells),
                intersection_first,
                intersection_weight,
            )
        ),
    )
    ring_a = jnp.where(flags[0:1] != 0, upstream_far, upstream)
    ring_b = jnp.where(flags[1:2] != 0, upstream_far, upstream)
    ring = jnp.concatenate([packed, halo_far], axis=0)
    at = 2
    for masks in groups(sectors):
        on_a, on_b, to_a = (flags[at + k : at + k + 1] for k in range(3))
        arrived = [
            exchange(
                jnp.concatenate([jnp.where(to_a == mask, ring_a, ring_b), ring], axis=0), sectors, mask
            )
            for mask in masks
        ]
        for mask, values in zip(masks, arrived):
            ring_a = jnp.where(on_a == mask, values[:count], ring_a)
            ring_b = jnp.where(on_b == mask, values[:count], ring_b)
        ring = jnp.concatenate([ring] + [values[count:] for values in arrived], axis=0)
        at += 3
    ring = ring.reshape(top, 2, HALF, cells)
    halos = ring.reshape(sectors, HALF, cells)

    sweep, ends = call(
        functools.partial(source_kernel, sectors, levels),
        out_shape=(shape(FIELDS, lines, cells), shape(end_rows, cells)),
        in_specs=[VMEM] * 9,
        out_specs=(VMEM, VMEM),
    )(ring_a, ring_b, halos, flow, gain, source, coef, flags, scan)
    values = exchange(jnp.concatenate([ends, ring[:, 0].reshape(top * HALF, cells)], axis=0), sectors, top)
    ends = ends + values[:end_rows]
    maps = jnp.concatenate([ring[:, 0], values[end_rows:].reshape(top, HALF, cells)], axis=0)
    suffix, closing = call(
        functools.partial(closing_kernel, sectors),
        out_shape=(shape(36, HALF, LANES), shape(36, HALF, LANES)),
        in_specs=[VMEM],
        out_specs=(VMEM, VMEM),
    )(maps)
    for masks in groups(sectors):
        for values in [exchange(ends, sectors, mask) for mask in masks]:
            ends = ends + values
    new_state = call(
        functools.partial(finish_kernel, sectors, levels),
        out_shape=shape(FIELDS, lines, cells),
        in_specs=[VMEM] * 6,
        out_specs=VMEM,
    )(ends, suffix, closing, flow, scan, sweep)
    return new_state.reshape(flow_state.shape)


def solution(mesh):
    return jax.shard_map(
        functools.partial(shards, mesh.shape["azim"], mesh.shape["row"]),
        mesh=mesh,
        in_specs=(
            P(None, None, "row", "azim"),
            P(None, None, "row", "azim"),
            P(None, "row", "azim"),
            P(),
            P(),
            P(None, None, None, "row", "azim"),
            P(None, None, None, "row", "azim"),
            P("row", "azim"),
            P("row", "azim"),
        ),
        out_specs=P(None, None, "row", "azim"),
        check_vma=False,
    )
```

```python
import functools

import jax
import jax.numpy as jnp
from jax import lax
from jax.experimental import pallas as pl
from jax.experimental.pallas import tpu as pltpu
from jax.sharding import PartitionSpec as P

FIELDS = 6
LANES = 128
HALF = 8
HALO = 72
JST_SECOND = 0.5
JST_FOURTH = 1.0 / 32.0
TIME_FACTOR = 1.5
VMEM = pl.BlockSpec(memory_space=pltpu.VMEM)
HBM = pl.BlockSpec(memory_space=pltpu.HBM)


def lane_ids():
    return lax.broadcasted_iota(jnp.int32, (HALF, LANES), 1)


def roll_lanes(x, shift):
    shift = shift % LANES
    return x if isinstance(shift, int) and shift == 0 else pltpu.roll(x, shift, 1)


def rows(half):
    return pl.ds(half * HALF, HALF)


def packing(sectors):
    return LANES // (2 * sectors)


def product(left, right):
    out = []
    for f in range(FIELDS):
        for h in range(FIELDS):
            acc = left[f * FIELDS] * right[h]
            for g in range(1, FIELDS):
                acc = acc + left[f * FIELDS + g] * right[g * FIELDS + h]
            out.append(acc)
    return out


def matvec(matrix, vector):
    out = []
    for f in range(FIELDS):
        acc = matrix[f * FIELDS] * vector[0]
        for g in range(1, FIELDS):
            acc = acc + matrix[f * FIELDS + g] * vector[g]
        out.append(acc)
    return out


def pack_last_lane(values, lane, base, width):
    acc = jnp.zeros((HALF, LANES), jnp.float32)
    for entry, pair in enumerate(values):
        for half in range(2):
            target = base + width * entry + half
            acc = jnp.where(lane == target, roll_lanes(pair[half], target + 1), acc)
    return acc


def groups(sectors):
    bits = sectors.bit_length() - 1
    found = []
    for low in reversed(range(0, bits - 1, 2)):
        found.append((1 << low, 2 << low, 3 << low))
    return found


def routes(sectors, place, cell):
    turn = (cell // LANES - place) & (sectors - 1)
    turns = (turn, (turn + 1) & (sectors - 1))
    flags = []
    half = sectors // 2
    for k in turns:
        borrow = jnp.where((place & (half - 1)) < (k & (half - 1)), half, 0)
        flags.append((k & half) ^ borrow)
    for unit, _, _ in groups(sectors):
        span = 4 * unit - 1
        mine = place & span & -unit
        for k in turns:
            low = (place - k) & (unit - 1)
            flags.append(mine ^ ((mine + low + k) & span & -unit))
        flags.append(mine ^ ((place - turn) & span & -unit))
    return flags


def edges_kernel(flow_in, flow, outlet, halo, sem):
    copy = pltpu.make_async_copy(flow_in, flow, sem)
    copy.start()
    lane = lane_ids()
    sub = lax.broadcasted_iota(jnp.int32, (HALF, LANES), 0)
    copy.wait()
    acc = jnp.zeros((HALF, LANES), jnp.float32)
    for f in range(FIELDS):
        lower, upper = flow[f, rows(0), :], flow[f, rows(1), :]
        outlet[pl.ds(f * HALF, HALF), :] = jnp.where((sub & 3) >= 2, lower, pltpu.roll(upper, HALF - 2, 0))
        for half, u in enumerate((lower, upper)):
            start = HALO + 4 * (2 * f + half)
            acc = jnp.where((lane >= start) & (lane < start + 2), roll_lanes(u, start), acc)
            acc = jnp.where((lane >= start + 2) & (lane < start + 4), roll_lanes(u, start + 4), acc)
    halo[...] = acc


def prepare_kernel(
    sectors,
    levels,
    flow,
    halo,
    old_in,
    step_in,
    azf_in,
    axf_in,
    inverse_in,
    lower_in,
    first_in,
    weight_in,
    gain,
    source,
    coef,
    flags,
    packed,
    scan,
    old,
    step_size,
    azf,
    axf,
    inverse,
    lower,
    first,
    weight,
    sems,
):
    copies = [
        pltpu.make_async_copy(src, dst, sems.at[at])
        for at, (src, dst) in enumerate(
            (
                (inverse_in, inverse),
                (lower_in, lower),
                (old_in, old),
                (step_in, step_size),
                (azf_in, azf),
                (axf_in, axf),
                (first_in, first),
                (weight_in, weight),
            )
        )
    ]
    for copy in copies:
        copy.start()
    lane = lane_ids()
    place = lax.axis_index("azim")
    for copy in copies:
        copy.wait()
    row = lax.broadcasted_iota(jnp.int32, (1, LANES), 1) * 0
    cell = row + jnp.broadcast_to(first[:, 0:1], (1, LANES))
    for at, flag in enumerate(routes(sectors, row + place, cell)):
        flags[pl.ds(at, 1), :] = flag
    flags[pl.ds(flags.shape[0] - 1, 1), :] = cell & (LANES - 1)
    for f in range(FIELDS):
        for g in range(FIELDS):
            at = f * FIELDS + g
            coef[pl.ds(at, 1), :] = jnp.broadcast_to(azf[f : f + 1, g : g + 1], (1, LANES))
            coef[pl.ds(36 + at, 1), :] = jnp.broadcast_to(axf[f : f + 1, g : g + 1], (1, LANES))
    coef[pl.ds(72, 1), :] = (weight[...].astype(jnp.float32) + 0.5) / 8.0
    for half in range(2):
        left = [inverse[e, rows(half), :] for e in range(36)]
        right = [lower[e, rows(half), :] for e in range(36)]
        for e, value in enumerate(product(left, right)):
            scan[e, rows(half), :] = value
    for half in range(2):
        minus_step = -step_size[rows(half), :]
        scaled = [minus_step * inverse[e, rows(half), :] for e in range(36)]
        change = [TIME_FACTOR * (flow[f, rows(half), :] - old[f, rows(half), :]) for f in range(FIELDS)]
        for e in range(36):
            gain[e, rows(half), :] = scaled[e]
        for f, value in enumerate(matvec(scaled, change)):
            source[f, rows(half), :] = value
    for level in range(levels):
        step = 1 << level
        keep = lane < step
        for half in range(2):
            later = [scan[36 * level + e, rows(half), :] for e in range(36)]
            earlier = [roll_lanes(x, step) for x in later]
            for e, value in enumerate(product(later, earlier)):
                scan[36 * (level + 1) + e, rows(half), :] = jnp.where(keep, later[e], value)
    acc = pack_last_lane(
        [[scan[36 * levels + e, rows(half), :] for half in range(2)] for e in range(36)], lane, 0, 2
    )
    packed[...] = jnp.where(lane < HALO, acc, halo[...])


def jst_parts(u0, um1, um2, up1, up2):
    p0, pm1, pm2, pp1, pp2 = [1.0 + x[0] * x[0] for x in (u0, um1, um2, up1, up2)]

    def sensor(up, mid, down):
        return jnp.abs(up - 2.0 * mid + down) / (up + 2.0 * mid + down)

    mid = sensor(pp1, p0, pm1)
    e2r = JST_SECOND * jnp.maximum(mid, sensor(pp2, pp1, p0))
    e2l = JST_SECOND * jnp.maximum(sensor(p0, pm1, pm2), mid)
    e4r = jnp.maximum(0.0, JST_FOURTH - e2r)
    e4l = jnp.maximum(0.0, JST_FOURTH - e2l)
    central, faces = [], []
    for f in range(FIELDS):
        dr = up1[f] - u0[f]
        dl = u0[f] - um1[f]
        third_r = up2[f] - 3.0 * up1[f] + 3.0 * u0[f] - um1[f]
        third_l = up1[f] - 3.0 * u0[f] + 3.0 * um1[f] - um2[f]
        central.append(0.5 * (up1[f] - um1[f]))
        faces.append((e2r * dr - e4r * third_r) - (e2l * dl - e4l * third_l))
    return central, faces


def gathered_at(sectors, difference):
    at, count = 0, 1
    for unit, _, _ in groups(sectors):
        at = at + ((difference // unit) & 3) * count
        count *= 4
    return at


def halo_at(sectors, difference):
    return 2 * gathered_at(sectors, difference) + difference // (sectors // 2)


def map_at(sectors, difference):
    return gathered_at(sectors, difference) + (difference // (sectors // 2)) * (sectors // 2)


def residual_kernel(sectors, ring_a, ring_b, ring, flow, coef, flags, reach, base, residual_out, packed):
    lane = lane_ids()
    sub = lax.broadcasted_iota(jnp.int32, (HALF, LANES), 0)
    place = lax.axis_index("azim")
    row = lax.axis_index("row")
    left_pack = ring[halo_at(sectors, place ^ ((place + sectors - 1) & (sectors - 1)))]
    right_pack = ring[halo_at(sectors, place ^ ((place + 1) & (sectors - 1)))]
    shift = flags[flags.shape[0] - 1, 0]
    back = (LANES - shift) & (LANES - 1)

    def coefficient(at):
        return jnp.broadcast_to(coef[pl.ds(at, 1), :], (HALF, LANES))

    frac = coefficient(72)
    ghost = []
    for f in range(FIELDS):
        a = pltpu.roll(ring_a[pl.ds(f * HALF, HALF), :], back, 1)
        b = pltpu.roll(ring_b[pl.ds(f * HALF, HALF), :], back, 1)
        one = jnp.where(lane < LANES - shift, a, b)
        two = pltpu.roll(jnp.where(lane == 0, b, one), LANES - 1, 1)
        ghost.append(frac * one + (1.0 - frac) * two)
    halo = jnp.where((lane & 3) < 2, right_pack, left_pack)
    axial = sub % 4
    ends = [[None, None] for _ in range(FIELDS)]
    is_first_row = row == 0
    for half in range(2):
        u0 = [flow[f, rows(half), :] for f in range(FIELDS)]
        um1, um2, up1, up2 = [], [], [], []
        for f in range(FIELDS):
            start = HALO + 4 * (2 * f + half)
            edge = roll_lanes(halo, LANES - 2 - start)
            um1.append(jnp.where(lane < 1, roll_lanes(halo, -(start + 3)), roll_lanes(u0[f], 1)))
            um2.append(jnp.where(lane < 2, edge, roll_lanes(u0[f], 2)))
            up1.append(jnp.where(lane >= LANES - 1, roll_lanes(halo, LANES - 1 - start), roll_lanes(u0[f], -1)))
            up2.append(jnp.where(lane >= LANES - 2, edge, roll_lanes(u0[f], -2)))
        az_central, az_faces = jst_parts(u0, um1, um2, up1, up2)
        um1, um2, up1, up2 = [], [], [], []
        for f in range(FIELDS):
            g = ghost[f]
            spread = pltpu.roll(g, HALF - 2, 0) if half == 0 else g
            u = u0[f]
            down1 = pltpu.roll(u, 1, 0)
            down2 = pltpu.roll(u, 2, 0)
            lift1 = pltpu.roll(u, HALF - 1, 0)
            lift2 = pltpu.roll(u, HALF - 2, 0)
            same = jnp.where(axial == 0, u, down1)
            spread = jnp.where(is_first_row, same, spread)
            next_ghost = pltpu.roll(spread, HALF - 1, 0)
            um1.append(jnp.where(axial == 0, next_ghost, down1))
            um2.append(jnp.where(axial < 2, spread, down2))
            last1 = jnp.where(axial == 3, u, lift1)
            up1.append(last1)
            up2.append(jnp.where(axial == 3, u, jnp.where(axial == 2, lift1, lift2)))
        ax_central, ax_faces = jst_parts(u0, um1, um2, up1, up2)
        residual = []
        for f in range(FIELDS):
            acc = -(az_faces[f] + ax_faces[f])
            for g in range(FIELDS):
                at = f * FIELDS + g
                acc = acc + coefficient(at) * az_central[g] + coefficient(36 + at) * ax_central[g]
            residual.append(acc)
        for f in range(FIELDS):
            residual_out[f, rows(half), :] = residual[f]
        parts = matvec([reach[e, rows(half), :] for e in range(36)], residual)
        for f in range(FIELDS):
            ends[f][half] = jnp.sum(parts[f], axis=1, keepdims=True)
    per = packing(sectors)
    for first in range(0, FIELDS, per):
        acc = base[pl.ds(HALF * (first // per), HALF), :]
        for entry, pair in enumerate(ends[first : first + per]):
            for half in range(2):
                target = entry * 2 * sectors + half
                acc = jnp.where(lane == target, acc + jnp.broadcast_to(pair[half], (HALF, LANES)), acc)
        packed[pl.ds(HALF * (first // per), HALF), :] = roll_lanes(acc, 2 * place)


def reach_kernel(sectors, levels, scan, gain, source, reach, base, work):
    lane = lane_ids()
    one = [jnp.float32(1.0 if e % 7 == 0 else 0.0) for e in range(36)]
    for half in range(2):
        for e in range(36):
            work[e, rows(half), :] = scan[e, rows(half), :]
    for level in range(levels):
        step = 1 << level
        for half in range(2):
            here = [work[e, rows(half), :] for e in range(36)]
            later = [
                jnp.where(lane < LANES - step, roll_lanes(x, -step), one[e]) for e, x in enumerate(here)
            ]
            for e, value in enumerate(product(later, here)):
                work[e, rows(half), :] = value
    sums = [[None, None] for _ in range(FIELDS)]
    for half in range(2):
        after = [
            jnp.where(lane < LANES - 1, roll_lanes(work[e, rows(half), :], -1), one[e]) for e in range(36)
        ]
        for e, value in enumerate(product(after, [gain[e, rows(half), :] for e in range(36)])):
            reach[e, rows(half), :] = value
        for f, value in enumerate(matvec(after, [source[f, rows(half), :] for f in range(FIELDS)])):
            sums[f][half] = jnp.sum(value, axis=1, keepdims=True)
    per = packing(sectors)
    for first in range(0, FIELDS, per):
        acc = jnp.zeros((HALF, LANES), jnp.float32)
        for entry, pair in enumerate(sums[first : first + per]):
            for half in range(2):
                target = entry * 2 * sectors + half
                acc = jnp.where(lane == target, jnp.broadcast_to(pair[half], (HALF, LANES)), acc)
        base[pl.ds(HALF * (first // per), HALF), :] = acc


def sweep_kernel(levels, residual, gain, source, scan, sweep):
    lane = lane_ids()
    values = [[None, None] for _ in range(FIELDS)]
    for half in range(2):
        added = matvec(
            [gain[e, rows(half), :] for e in range(36)], [residual[f, rows(half), :] for f in range(FIELDS)]
        )
        for f in range(FIELDS):
            values[f][half] = source[f, rows(half), :] + added[f]
    for level in range(levels):
        step = 1 << level
        for half in range(2):
            before = [jnp.where(lane < step, 0.0, roll_lanes(values[f][half], step)) for f in range(FIELDS)]
            matrix = [scan[36 * level + e, rows(half), :] for e in range(36)]
            for f, gained in enumerate(matvec(matrix, before)):
                values[f][half] = values[f][half] + gained
    for f in range(FIELDS):
        for half in range(2):
            sweep[f, rows(half), :] = values[f][half]


def closing_kernel(sectors, ring, weights):
    lane = lane_ids()
    place = lax.axis_index("azim")
    width = 2 * sectors
    one = [jnp.float32(1.0 if e % 7 == 0 else 0.0) for e in range(36)]
    turned = []
    for t in range(sectors):
        at = map_at(sectors, place ^ ((place + t) & (sectors - 1)))
        turned.append(roll_lanes(ring[at], 2 * t))
    pair = lane >> 1
    maps = []
    for e in range(36):
        acc = turned[0]
        for t in range(1, sectors):
            acc = jnp.where(pair == (e + t) % (LANES // 2), turned[t], acc)
        maps.append(roll_lanes(acc, -2 * e))
    step = 2
    while step < width:
        later = [jnp.where(lane < width - step, roll_lanes(x, -step), one[e]) for e, x in enumerate(maps)]
        maps = product(later, maps)
        step *= 2
    suffix = [jnp.where(lane < width - 2, roll_lanes(maps[e], -2), one[e]) for e in range(36)]
    system = [[one[f * 6 + g] - maps[f * 6 + g] for g in range(6)] for f in range(6)]
    result = [[jnp.full((HALF, LANES), one[f * 6 + g]) for g in range(6)] for f in range(6)]
    for pivot in range(6):
        scale = 1.0 / system[pivot][pivot]
        for g in range(pivot + 1, 6):
            system[pivot][g] = system[pivot][g] * scale
        for g in range(pivot + 1):
            result[pivot][g] = result[pivot][g] * scale
        for f in range(6):
            if f == pivot:
                continue
            factor = system[f][pivot]
            for g in range(pivot + 1, 6):
                system[f][g] = system[f][g] - factor * system[pivot][g]
            for g in range(pivot + 1):
                result[f][g] = result[f][g] - factor * result[pivot][g]
    closing = []
    for e in range(36):
        value = jnp.where(lane < 2, result[e // 6][e % 6], 0.0)
        step = 2
        while step < width:
            value = value + roll_lanes(value, step)
            step *= 2
        closing.append(value)
    start = product(closing, suffix)
    per = packing(sectors)
    turn = 2 * place
    crossed = (lane & (width - 1)) < turn
    for f in range(FIELDS):
        for first in range(0, FIELDS, per):
            acc = jnp.zeros((HALF, LANES), jnp.float32)
            for entry in range(min(per, FIELDS - first)):
                at = entry * width
                inside = (lane >= at) & (lane < at + width)
                acc = jnp.where(inside, roll_lanes(start[f * 6 + first + entry], at), acc)
            ahead = pltpu.roll(acc, turn, 1)
            behind = pltpu.roll(acc, lax.rem(LANES + turn - width, LANES), 1)
            row = HALF * (f * pl.cdiv(FIELDS, per) + first // per)
            weights[pl.ds(row, HALF), :] = jnp.where(crossed, behind, ahead)


def finish_kernel(sectors, levels, gathered, weights, flow, scan, sweep, out):
    lane = lane_ids()
    count = pl.cdiv(FIELDS, packing(sectors))
    begin = [[None] * FIELDS for _ in range(2)]
    for f in range(FIELDS):
        acc = None
        for at in range(count):
            term = weights[pl.ds(HALF * (f * count + at), HALF), :] * gathered[pl.ds(HALF * at, HALF), :]
            acc = term if acc is None else acc + term
        for half in range(2):
            total = jnp.sum(jnp.where((lane & 1) == half, acc, 0.0), axis=1, keepdims=True)
            begin[half][f] = jnp.broadcast_to(total, (HALF, LANES))
    for half in range(2):
        gained = matvec([scan[36 * levels + e, rows(half), :] for e in range(36)], begin[half])
        for f in range(FIELDS):
            out[f, rows(half), :] = flow[f, rows(half), :] + (gained[f] + sweep[f, rows(half), :])


def exchange(values, sectors, mask):
    return lax.ppermute(values, "azim", [(i, i ^ mask) for i in range(sectors)])


def from_upstream(values, sectors, row_count, mask):
    return lax.ppermute(
        values,
        ("azim", "row"),
        [
            (i * row_count + r, (i ^ mask) * row_count + (r + 1) % row_count)
            for i in range(sectors)
            for r in range(row_count)
        ],
    )


def in_hbm(x):
    return pltpu.with_memory_space_constraint(x, pltpu.HBM)


def shape(*dims):
    return jax.ShapeDtypeStruct(dims, jnp.float32)


def shards(
    sectors,
    row_count,
    flow_state,
    old_state,
    local_step,
    azim_flux,
    axial_flux,
    block_inverse,
    lower_block,
    intersection_first,
    intersection_weight,
):
    radial, axial, cells = flow_state.shape[1:]
    lines = radial * axial
    levels = cells.bit_length() - 1
    end_rows = HALF * pl.cdiv(FIELDS, packing(sectors))
    flag_rows = HALF * pl.cdiv(3 * sectors.bit_length(), HALF)
    count = FIELDS * HALF
    call = functools.partial(
        pl.pallas_call, compiler_params=pltpu.CompilerParams(vmem_limit_bytes=16 << 20)
    )

    flow, outlet, halo = call(
        edges_kernel,
        out_shape=(shape(FIELDS, lines, cells), shape(count, cells), shape(HALF, cells)),
        in_specs=[HBM],
        out_specs=(VMEM,) * 3,
        scratch_shapes=[pltpu.SemaphoreType.DMA(())],
    )(in_hbm(flow_state.reshape(FIELDS, lines, cells)))
    top = sectors // 2
    upstream_far = from_upstream(outlet, sectors, row_count, top)
    halo_far = exchange(halo, sectors, top)
    upstream = from_upstream(outlet, sectors, row_count, 0)
    gain, source, coef, flags, packed, scan = call(
        functools.partial(prepare_kernel, sectors, levels),
        out_shape=(
            shape(36, lines, cells),
            shape(FIELDS, lines, cells),
            shape(80, cells),
            jax.ShapeDtypeStruct((flag_rows, cells), jnp.int32),
            shape(HALF, cells),
            shape(36 * (levels + 1), lines, cells),
        ),
        in_specs=[VMEM] * 2 + [HBM] * 8,
        out_specs=(VMEM,) * 6,
        scratch_shapes=[
            pltpu.VMEM((FIELDS, lines, cells), jnp.float32),
            pltpu.VMEM((lines, cells), jnp.float32),
            pltpu.VMEM((FIELDS, FIELDS), jnp.float32),
            pltpu.VMEM((FIELDS, FIELDS), jnp.float32),
            pltpu.VMEM((36, lines, cells), jnp.float32),
            pltpu.VMEM((36, lines, cells), jnp.float32),
            pltpu.VMEM((1, cells), jnp.int32),
            pltpu.VMEM((1, cells), jnp.int32),
            pltpu.SemaphoreType.DMA((8,)),
        ],
    )(
        flow,
        halo,
        *(
            in_hbm(x)
            for x in (
                old_state.reshape(FIELDS, lines, cells),
                local_step.reshape(lines, cells),
                azim_flux,
                axial_flux,
                block_inverse.reshape(36, lines, cells),
                lower_block.reshape(36, lines, cells),
                intersection_first,
                intersection_weight,
            )
        ),
    )
    ring_a = jnp.where(flags[0:1] != 0, upstream_far, upstream)
    ring_b = jnp.where(flags[1:2] != 0, upstream_far, upstream)
    ring = jnp.concatenate([packed, halo_far], axis=0)
    at = 2
    for masks in groups(sectors):
        on_a, on_b, to_a = (flags[at + k : at + k + 1] for k in range(3))
        arrived = []
        for mask in masks:
            sent = jnp.concatenate([jnp.where(to_a == mask, ring_a, ring_b), ring], axis=0)
            arrived.append(exchange(sent, sectors, mask))
        for mask, values in zip(masks, arrived):
            ring_a = jnp.where(on_a == mask, values[:count], ring_a)
            ring_b = jnp.where(on_b == mask, values[:count], ring_b)
        ring = jnp.concatenate([ring] + [values[count:] for values in arrived], axis=0)
        at += 3
    ring = ring.reshape(top, 2, HALF, cells)
    halos = ring.reshape(sectors, HALF, cells)

    reach, base = call(
        functools.partial(reach_kernel, sectors, levels),
        out_shape=(shape(36, lines, cells), shape(end_rows, cells)),
        in_specs=[VMEM] * 3,
        out_specs=(VMEM, VMEM),
        scratch_shapes=[pltpu.VMEM((36, lines, cells), jnp.float32)],
    )(scan, gain, source)
    residual, ends = call(
        functools.partial(residual_kernel, sectors),
        out_shape=(shape(FIELDS, lines, cells), shape(end_rows, cells)),
        in_specs=[VMEM] * 8,
        out_specs=(VMEM, VMEM),
    )(ring_a, ring_b, halos, flow, coef, flags, reach, base)
    sweep = call(
        functools.partial(sweep_kernel, levels),
        out_shape=shape(FIELDS, lines, cells),
        in_specs=[VMEM] * 4,
        out_specs=VMEM,
        cost_estimate=pl.CostEstimate(flops=1 << 20, bytes_accessed=1 << 21, transcendentals=0),
    )(residual, gain, source, scan)
    values = exchange(jnp.concatenate([ends, ring[:, 0].reshape(top * HALF, cells)], axis=0), sectors, top)
    ends = ends + values[:end_rows]
    maps = jnp.concatenate([ring[:, 0], values[end_rows:].reshape(top, HALF, cells)], axis=0)
    weights = call(
        functools.partial(closing_kernel, sectors),
        out_shape=shape(FIELDS * end_rows, cells),
        in_specs=[VMEM],
        out_specs=VMEM,
    )(maps)
    for masks in groups(sectors):
        for values in [exchange(ends, sectors, mask) for mask in masks]:
            ends = ends + values
    new_state = call(
        functools.partial(finish_kernel, sectors, levels),
        out_shape=shape(FIELDS, lines, cells),
        in_specs=[VMEM] * 5,
        out_specs=VMEM,
    )(ends, weights, flow, scan, sweep)
    return new_state.reshape(flow_state.shape)


def solution(mesh):
    return jax.shard_map(
        functools.partial(shards, mesh.shape["azim"], mesh.shape["row"]),
        mesh=mesh,
        in_specs=(
            P(None, None, "row", "azim"),
            P(None, None, "row", "azim"),
            P(None, "row", "azim"),
            P(),
            P(),
            P(None, None, None, "row", "azim"),
            P(None, None, None, "row", "azim"),
            P("row", "azim"),
            P("row", "azim"),
        ),
        out_specs=P(None, None, "row", "azim"),
        check_vma=False,
    )
```

```python
import functools

import jax
import jax.numpy as jnp
from jax import lax
from jax.experimental import pallas as pl
from jax.experimental.pallas import tpu as pltpu
from jax.sharding import PartitionSpec as P

FIELDS = 6
LANES = 128
HALF = 8
HALO = 72
JST_SECOND = 0.5
JST_FOURTH = 1.0 / 32.0
TIME_FACTOR = 1.5
VMEM = pl.BlockSpec(memory_space=pltpu.VMEM)
HBM = pl.BlockSpec(memory_space=pltpu.HBM)


def lane_ids():
    return lax.broadcasted_iota(jnp.int32, (HALF, LANES), 1)


def roll_lanes(x, shift):
    shift = shift % LANES
    return x if isinstance(shift, int) and shift == 0 else pltpu.roll(x, shift, 1)


def rows(half):
    return pl.ds(half * HALF, HALF)


def packing(sectors):
    return LANES // (2 * sectors)


def product(left, right):
    out = []
    for f in range(FIELDS):
        for h in range(FIELDS):
            acc = left[f * FIELDS] * right[h]
            for g in range(1, FIELDS):
                acc = acc + left[f * FIELDS + g] * right[g * FIELDS + h]
            out.append(acc)
    return out


def matvec(matrix, vector):
    out = []
    for f in range(FIELDS):
        acc = matrix[f * FIELDS] * vector[0]
        for g in range(1, FIELDS):
            acc = acc + matrix[f * FIELDS + g] * vector[g]
        out.append(acc)
    return out


def pack_last_lane(values, lane, base, width):
    acc = jnp.zeros((HALF, LANES), jnp.float32)
    for entry, pair in enumerate(values):
        for half in range(2):
            target = base + width * entry + half
            acc = jnp.where(lane == target, roll_lanes(pair[half], target + 1), acc)
    return acc


def groups(sectors):
    bits = sectors.bit_length() - 1
    found = []
    for low in reversed(range(0, bits - 1, 2)):
        found.append((1 << low, 2 << low, 3 << low))
    return found


def routes(sectors, place, cell):
    turn = (cell // LANES - place) & (sectors - 1)
    turns = (turn, (turn + 1) & (sectors - 1))
    flags = []
    half = sectors // 2
    for k in turns:
        borrow = jnp.where((place & (half - 1)) < (k & (half - 1)), half, 0)
        flags.append((k & half) ^ borrow)
    for unit, _, _ in groups(sectors):
        span = 4 * unit - 1
        mine = place & span & -unit
        for k in turns:
            low = (place - k) & (unit - 1)
            flags.append(mine ^ ((mine + low + k) & span & -unit))
        flags.append(mine ^ ((place - turn) & span & -unit))
    return flags


def edges_kernel(flow_in, flow, outlet, halo, sem):
    copy = pltpu.make_async_copy(flow_in, flow, sem)
    copy.start()
    lane = lane_ids()
    sub = lax.broadcasted_iota(jnp.int32, (HALF, LANES), 0)
    copy.wait()
    acc = jnp.zeros((HALF, LANES), jnp.float32)
    for f in range(FIELDS):
        lower, upper = flow[f, rows(0), :], flow[f, rows(1), :]
        outlet[pl.ds(f * HALF, HALF), :] = jnp.where((sub & 3) >= 2, lower, pltpu.roll(upper, HALF - 2, 0))
        for half, u in enumerate((lower, upper)):
            start = HALO + 4 * (2 * f + half)
            acc = jnp.where((lane >= start) & (lane < start + 2), roll_lanes(u, start), acc)
            acc = jnp.where((lane >= start + 2) & (lane < start + 4), roll_lanes(u, start + 4), acc)
    halo[...] = acc


def prepare_kernel(
    sectors,
    levels,
    flow,
    halo,
    old_in,
    step_in,
    azf_in,
    axf_in,
    inverse_in,
    lower_in,
    first_in,
    weight_in,
    gain,
    source,
    coef,
    flags,
    packed,
    scan,
    old,
    step_size,
    azf,
    axf,
    inverse,
    lower,
    first,
    weight,
    sems,
):
    copies = [
        pltpu.make_async_copy(src, dst, sems.at[at])
        for at, (src, dst) in enumerate(
            (
                (inverse_in, inverse),
                (lower_in, lower),
                (old_in, old),
                (step_in, step_size),
                (azf_in, azf),
                (axf_in, axf),
                (first_in, first),
                (weight_in, weight),
            )
        )
    ]
    for copy in copies:
        copy.start()
    lane = lane_ids()
    place = lax.axis_index("azim")
    for copy in copies:
        copy.wait()
    row = lax.broadcasted_iota(jnp.int32, (1, LANES), 1) * 0
    cell = row + jnp.broadcast_to(first[:, 0:1], (1, LANES))
    for at, flag in enumerate(routes(sectors, row + place, cell)):
        flags[pl.ds(at, 1), :] = flag
    flags[pl.ds(flags.shape[0] - 1, 1), :] = cell & (LANES - 1)
    for f in range(FIELDS):
        for g in range(FIELDS):
            at = f * FIELDS + g
            coef[pl.ds(at, 1), :] = jnp.broadcast_to(azf[f : f + 1, g : g + 1], (1, LANES))
            coef[pl.ds(36 + at, 1), :] = jnp.broadcast_to(axf[f : f + 1, g : g + 1], (1, LANES))
    coef[pl.ds(72, 1), :] = (weight[...].astype(jnp.float32) + 0.5) / 8.0
    for half in range(2):
        left = [inverse[e, rows(half), :] for e in range(36)]
        right = [lower[e, rows(half), :] for e in range(36)]
        for e, value in enumerate(product(left, right)):
            scan[e, rows(half), :] = value
    for half in range(2):
        minus_step = -step_size[rows(half), :]
        scaled = [minus_step * inverse[e, rows(half), :] for e in range(36)]
        change = [TIME_FACTOR * (flow[f, rows(half), :] - old[f, rows(half), :]) for f in range(FIELDS)]
        for e in range(36):
            gain[e, rows(half), :] = scaled[e]
        for f, value in enumerate(matvec(scaled, change)):
            source[f, rows(half), :] = value
    for level in range(levels):
        step = 1 << level
        keep = lane < step
        for half in range(2):
            later = [scan[36 * level + e, rows(half), :] for e in range(36)]
            earlier = [roll_lanes(x, step) for x in later]
            for e, value in enumerate(product(later, earlier)):
                scan[36 * (level + 1) + e, rows(half), :] = jnp.where(keep, later[e], value)
    acc = pack_last_lane(
        [[scan[36 * levels + e, rows(half), :] for half in range(2)] for e in range(36)], lane, 0, 2
    )
    packed[...] = jnp.where(lane < HALO, acc, halo[...])


def jst_parts(u0, um1, um2, up1, up2):
    p0, pm1, pm2, pp1, pp2 = [1.0 + x[0] * x[0] for x in (u0, um1, um2, up1, up2)]

    def sensor(up, mid, down):
        return jnp.abs(up - 2.0 * mid + down) / (up + 2.0 * mid + down)

    mid = sensor(pp1, p0, pm1)
    e2r = JST_SECOND * jnp.maximum(mid, sensor(pp2, pp1, p0))
    e2l = JST_SECOND * jnp.maximum(sensor(p0, pm1, pm2), mid)
    e4r = jnp.maximum(0.0, JST_FOURTH - e2r)
    e4l = jnp.maximum(0.0, JST_FOURTH - e2l)
    central, faces = [], []
    for f in range(FIELDS):
        dr = up1[f] - u0[f]
        dl = u0[f] - um1[f]
        third_r = up2[f] - 3.0 * up1[f] + 3.0 * u0[f] - um1[f]
        third_l = up1[f] - 3.0 * u0[f] + 3.0 * um1[f] - um2[f]
        central.append(0.5 * (up1[f] - um1[f]))
        faces.append((e2r * dr - e4r * third_r) - (e2l * dl - e4l * third_l))
    return central, faces


def gathered_at(sectors, difference):
    at, count = 0, 1
    for unit, _, _ in groups(sectors):
        at = at + ((difference // unit) & 3) * count
        count *= 4
    return at


def halo_at(sectors, difference):
    return 2 * gathered_at(sectors, difference) + difference // (sectors // 2)


def map_at(sectors, difference):
    return gathered_at(sectors, difference) + (difference // (sectors // 2)) * (sectors // 2)


def residual_kernel(sectors, ring_a, ring_b, ring, flow, coef, flags, reach, base, residual_out, packed):
    lane = lane_ids()
    sub = lax.broadcasted_iota(jnp.int32, (HALF, LANES), 0)
    place = lax.axis_index("azim")
    row = lax.axis_index("row")
    left_pack = ring[halo_at(sectors, place ^ ((place + sectors - 1) & (sectors - 1)))]
    right_pack = ring[halo_at(sectors, place ^ ((place + 1) & (sectors - 1)))]
    shift = flags[flags.shape[0] - 1, 0]
    back = (LANES - shift) & (LANES - 1)

    def coefficient(at):
        return jnp.broadcast_to(coef[pl.ds(at, 1), :], (HALF, LANES))

    frac = coefficient(72)
    ghost = []
    for f in range(FIELDS):
        a = pltpu.roll(ring_a[pl.ds(f * HALF, HALF), :], back, 1)
        b = pltpu.roll(ring_b[pl.ds(f * HALF, HALF), :], back, 1)
        one = jnp.where(lane < LANES - shift, a, b)
        two = pltpu.roll(jnp.where(lane == 0, b, one), LANES - 1, 1)
        ghost.append(frac * one + (1.0 - frac) * two)
    halo = jnp.where((lane & 3) < 2, right_pack, left_pack)
    axial = sub % 4
    ends = [[None, None] for _ in range(FIELDS)]
    is_first_row = row == 0
    for half in range(2):
        u0 = [flow[f, rows(half), :] for f in range(FIELDS)]
        um1, um2, up1, up2 = [], [], [], []
        for f in range(FIELDS):
            start = HALO + 4 * (2 * f + half)
            edge = roll_lanes(halo, LANES - 2 - start)
            um1.append(jnp.where(lane < 1, roll_lanes(halo, -(start + 3)), roll_lanes(u0[f], 1)))
            um2.append(jnp.where(lane < 2, edge, roll_lanes(u0[f], 2)))
            up1.append(jnp.where(lane >= LANES - 1, roll_lanes(halo, LANES - 1 - start), roll_lanes(u0[f], -1)))
            up2.append(jnp.where(lane >= LANES - 2, edge, roll_lanes(u0[f], -2)))
        az_central, az_faces = jst_parts(u0, um1, um2, up1, up2)
        um1, um2, up1, up2 = [], [], [], []
        for f in range(FIELDS):
            g = ghost[f]
            spread = pltpu.roll(g, HALF - 2, 0) if half == 0 else g
            u = u0[f]
            down1 = pltpu.roll(u, 1, 0)
            down2 = pltpu.roll(u, 2, 0)
            lift1 = pltpu.roll(u, HALF - 1, 0)
            lift2 = pltpu.roll(u, HALF - 2, 0)
            same = jnp.where(axial == 0, u, down1)
            spread = jnp.where(is_first_row, same, spread)
            next_ghost = pltpu.roll(spread, HALF - 1, 0)
            um1.append(jnp.where(axial == 0, next_ghost, down1))
            um2.append(jnp.where(axial < 2, spread, down2))
            last1 = jnp.where(axial == 3, u, lift1)
            up1.append(last1)
            up2.append(jnp.where(axial == 3, u, jnp.where(axial == 2, lift1, lift2)))
        ax_central, ax_faces = jst_parts(u0, um1, um2, up1, up2)
        residual = []
        for f in range(FIELDS):
            acc = -(az_faces[f] + ax_faces[f])
            for g in range(FIELDS):
                at = f * FIELDS + g
                acc = acc + coefficient(at) * az_central[g] + coefficient(36 + at) * ax_central[g]
            residual.append(acc)
        for f in range(FIELDS):
            residual_out[f, rows(half), :] = residual[f]
        parts = matvec([reach[e, rows(half), :] for e in range(36)], residual)
        for f in range(FIELDS):
            ends[f][half] = jnp.sum(parts[f], axis=1, keepdims=True)
    per = packing(sectors)
    for first in range(0, FIELDS, per):
        acc = base[pl.ds(HALF * (first // per), HALF), :]
        for entry, pair in enumerate(ends[first : first + per]):
            for half in range(2):
                target = entry * 2 * sectors + half
                acc = jnp.where(lane == target, acc + jnp.broadcast_to(pair[half], (HALF, LANES)), acc)
        packed[pl.ds(HALF * (first // per), HALF), :] = roll_lanes(acc, 2 * place)


def reach_kernel(sectors, levels, scan, gain, source, reach, base, work):
    lane = lane_ids()
    one = [jnp.float32(1.0 if e % 7 == 0 else 0.0) for e in range(36)]
    for half in range(2):
        for e in range(36):
            work[e, rows(half), :] = scan[e, rows(half), :]
    for level in range(levels):
        step = 1 << level
        for half in range(2):
            here = [work[e, rows(half), :] for e in range(36)]
            later = [
                jnp.where(lane < LANES - step, roll_lanes(x, -step), one[e]) for e, x in enumerate(here)
            ]
            for e, value in enumerate(product(later, here)):
                work[e, rows(half), :] = value
    sums = [[None, None] for _ in range(FIELDS)]
    for half in range(2):
        after = [
            jnp.where(lane < LANES - 1, roll_lanes(work[e, rows(half), :], -1), one[e]) for e in range(36)
        ]
        for e, value in enumerate(product(after, [gain[e, rows(half), :] for e in range(36)])):
            reach[e, rows(half), :] = value
        for f, value in enumerate(matvec(after, [source[f, rows(half), :] for f in range(FIELDS)])):
            sums[f][half] = jnp.sum(value, axis=1, keepdims=True)
    per = packing(sectors)
    for first in range(0, FIELDS, per):
        acc = jnp.zeros((HALF, LANES), jnp.float32)
        for entry, pair in enumerate(sums[first : first + per]):
            for half in range(2):
                target = entry * 2 * sectors + half
                acc = jnp.where(lane == target, jnp.broadcast_to(pair[half], (HALF, LANES)), acc)
        base[pl.ds(HALF * (first // per), HALF), :] = acc


def sweep_kernel(levels, residual, gain, source, scan, sweep):
    lane = lane_ids()
    values = [[None, None] for _ in range(FIELDS)]
    for half in range(2):
        added = matvec(
            [gain[e, rows(half), :] for e in range(36)], [residual[f, rows(half), :] for f in range(FIELDS)]
        )
        for f in range(FIELDS):
            values[f][half] = source[f, rows(half), :] + added[f]
    for level in range(levels):
        step = 1 << level
        for half in range(2):
            before = [jnp.where(lane < step, 0.0, roll_lanes(values[f][half], step)) for f in range(FIELDS)]
            matrix = [scan[36 * level + e, rows(half), :] for e in range(36)]
            for f, gained in enumerate(matvec(matrix, before)):
                values[f][half] = values[f][half] + gained
    for f in range(FIELDS):
        for half in range(2):
            sweep[f, rows(half), :] = values[f][half]


def closing_kernel(sectors, ring, weights):
    lane = lane_ids()
    place = lax.axis_index("azim")
    width = 2 * sectors
    one = [jnp.float32(1.0 if e % 7 == 0 else 0.0) for e in range(36)]
    turned = []
    for t in range(sectors):
        at = map_at(sectors, place ^ ((place + t) & (sectors - 1)))
        turned.append(roll_lanes(ring[at], 2 * t))
    pair = lane >> 1
    maps = []
    for e in range(36):
        acc = turned[0]
        for t in range(1, sectors):
            acc = jnp.where(pair == (e + t) % (LANES // 2), turned[t], acc)
        maps.append(roll_lanes(acc, -2 * e))
    step = 2
    while step < width:
        later = [jnp.where(lane < width - step, roll_lanes(x, -step), one[e]) for e, x in enumerate(maps)]
        maps = product(later, maps)
        step *= 2
    suffix = [jnp.where(lane < width - 2, roll_lanes(maps[e], -2), one[e]) for e in range(36)]
    system = [[one[f * 6 + g] - maps[f * 6 + g] for g in range(6)] for f in range(6)]
    result = [[jnp.full((HALF, LANES), one[f * 6 + g]) for g in range(6)] for f in range(6)]
    for pivot in range(6):
        scale = 1.0 / system[pivot][pivot]
        for g in range(pivot + 1, 6):
            system[pivot][g] = system[pivot][g] * scale
        for g in range(pivot + 1):
            result[pivot][g] = result[pivot][g] * scale
        for f in range(6):
            if f == pivot:
                continue
            factor = system[f][pivot]
            for g in range(pivot + 1, 6):
                system[f][g] = system[f][g] - factor * system[pivot][g]
            for g in range(pivot + 1):
                result[f][g] = result[f][g] - factor * result[pivot][g]
    closing = []
    for e in range(36):
        value = jnp.where(lane < 2, result[e // 6][e % 6], 0.0)
        step = 2
        while step < width:
            value = value + roll_lanes(value, step)
            step *= 2
        closing.append(value)
    start = product(closing, suffix)
    per = packing(sectors)
    turn = 2 * place
    crossed = (lane & (width - 1)) < turn
    for f in range(FIELDS):
        for first in range(0, FIELDS, per):
            acc = jnp.zeros((HALF, LANES), jnp.float32)
            for entry in range(min(per, FIELDS - first)):
                at = entry * width
                inside = (lane >= at) & (lane < at + width)
                acc = jnp.where(inside, roll_lanes(start[f * 6 + first + entry], at), acc)
            ahead = pltpu.roll(acc, turn, 1)
            behind = pltpu.roll(acc, lax.rem(LANES + turn - width, LANES), 1)
            row = HALF * (f * pl.cdiv(FIELDS, per) + first // per)
            weights[pl.ds(row, HALF), :] = jnp.where(crossed, behind, ahead)


def finish_kernel(sectors, levels, gathered, weights, flow, scan, sweep, out):
    lane = lane_ids()
    count = pl.cdiv(FIELDS, packing(sectors))
    begin = [[None] * FIELDS for _ in range(2)]
    for f in range(FIELDS):
        acc = None
        for at in range(count):
            term = weights[pl.ds(HALF * (f * count + at), HALF), :] * gathered[pl.ds(HALF * at, HALF), :]
            acc = term if acc is None else acc + term
        for half in range(2):
            total = jnp.sum(jnp.where((lane & 1) == half, acc, 0.0), axis=1, keepdims=True)
            begin[half][f] = jnp.broadcast_to(total, (HALF, LANES))
    for half in range(2):
        gained = matvec([scan[36 * levels + e, rows(half), :] for e in range(36)], begin[half])
        for f in range(FIELDS):
            out[f, rows(half), :] = flow[f, rows(half), :] + (gained[f] + sweep[f, rows(half), :])


def exchange(values, sectors, mask):
    return lax.ppermute(values, "azim", [(i, i ^ mask) for i in range(sectors)])


def from_upstream(values, sectors, row_count, mask):
    return lax.ppermute(
        values,
        ("azim", "row"),
        [
            (i * row_count + r, (i ^ mask) * row_count + (r + 1) % row_count)
            for i in range(sectors)
            for r in range(row_count)
        ],
    )


def in_hbm(x):
    return pltpu.with_memory_space_constraint(x, pltpu.HBM)


def shape(*dims):
    return jax.ShapeDtypeStruct(dims, jnp.float32)


def shards(
    sectors,
    row_count,
    flow_state,
    old_state,
    local_step,
    azim_flux,
    axial_flux,
    block_inverse,
    lower_block,
    intersection_first,
    intersection_weight,
):
    radial, axial, cells = flow_state.shape[1:]
    lines = radial * axial
    levels = cells.bit_length() - 1
    end_rows = HALF * pl.cdiv(FIELDS, packing(sectors))
    flag_rows = HALF * pl.cdiv(3 * sectors.bit_length(), HALF)
    count = FIELDS * HALF
    call = functools.partial(
        pl.pallas_call, compiler_params=pltpu.CompilerParams(vmem_limit_bytes=16 << 20)
    )

    flow, outlet, halo = call(
        edges_kernel,
        out_shape=(shape(FIELDS, lines, cells), shape(count, cells), shape(HALF, cells)),
        in_specs=[HBM],
        out_specs=(VMEM,) * 3,
        scratch_shapes=[pltpu.SemaphoreType.DMA(())],
    )(in_hbm(flow_state.reshape(FIELDS, lines, cells)))
    top = sectors // 2
    upstream_far = from_upstream(outlet, sectors, row_count, top)
    halo_far = exchange(halo, sectors, top)
    upstream = from_upstream(outlet, sectors, row_count, 0)
    gain, source, coef, flags, packed, scan = call(
        functools.partial(prepare_kernel, sectors, levels),
        out_shape=(
            shape(36, lines, cells),
            shape(FIELDS, lines, cells),
            shape(80, cells),
            jax.ShapeDtypeStruct((flag_rows, cells), jnp.int32),
            shape(HALF, cells),
            shape(36 * (levels + 1), lines, cells),
        ),
        in_specs=[VMEM] * 2 + [HBM] * 8,
        out_specs=(VMEM,) * 6,
        scratch_shapes=[
            pltpu.VMEM((FIELDS, lines, cells), jnp.float32),
            pltpu.VMEM((lines, cells), jnp.float32),
            pltpu.VMEM((FIELDS, FIELDS), jnp.float32),
            pltpu.VMEM((FIELDS, FIELDS), jnp.float32),
            pltpu.VMEM((36, lines, cells), jnp.float32),
            pltpu.VMEM((36, lines, cells), jnp.float32),
            pltpu.VMEM((1, cells), jnp.int32),
            pltpu.VMEM((1, cells), jnp.int32),
            pltpu.SemaphoreType.DMA((8,)),
        ],
    )(
        flow,
        halo,
        *(
            in_hbm(x)
            for x in (
                old_state.reshape(FIELDS, lines, cells),
                local_step.reshape(lines, cells),
                azim_flux,
                axial_flux,
                block_inverse.reshape(36, lines, cells),
                lower_block.reshape(36, lines, cells),
                intersection_first,
                intersection_weight,
            )
        ),
    )
    ring_a = jnp.where(flags[0:1] != 0, upstream_far, upstream)
    ring_b = jnp.where(flags[1:2] != 0, upstream_far, upstream)
    ring = jnp.concatenate([packed, halo_far], axis=0)
    at = 2
    for masks in groups(sectors):
        on_a, on_b, to_a = (flags[at + k : at + k + 1] for k in range(3))
        arrived = []
        for mask in masks:
            sent = jnp.concatenate([jnp.where(to_a == mask, ring_a, ring_b), ring], axis=0)
            arrived.append(exchange(sent, sectors, mask))
        for mask, values in zip(masks, arrived):
            ring_a = jnp.where(on_a == mask, values[:count], ring_a)
            ring_b = jnp.where(on_b == mask, values[:count], ring_b)
        ring = jnp.concatenate([ring] + [values[count:] for values in arrived], axis=0)
        at += 3
    ring = ring.reshape(top, 2, HALF, cells)
    halos = ring.reshape(sectors, HALF, cells)

    reach, base = call(
        functools.partial(reach_kernel, sectors, levels),
        out_shape=(shape(36, lines, cells), shape(end_rows, cells)),
        in_specs=[VMEM] * 3,
        out_specs=(VMEM, VMEM),
        scratch_shapes=[pltpu.VMEM((36, lines, cells), jnp.float32)],
    )(scan, gain, source)
    residual, ends = call(
        functools.partial(residual_kernel, sectors),
        out_shape=(shape(FIELDS, lines, cells), shape(end_rows, cells)),
        in_specs=[VMEM] * 8,
        out_specs=(VMEM, VMEM),
    )(ring_a, ring_b, halos, flow, coef, flags, reach, base)
    sweep = call(
        functools.partial(sweep_kernel, levels),
        out_shape=shape(FIELDS, lines, cells),
        in_specs=[VMEM] * 4,
        out_specs=VMEM,
    )(residual, gain, source, scan)
    across = exchange(ends, sectors, top)
    others = exchange(ring[:, 0].reshape(top * HALF, cells), sectors, top)
    ends = ends + across
    maps = jnp.concatenate([ring[:, 0], others.reshape(top, HALF, cells)], axis=0)
    weights = call(
        functools.partial(closing_kernel, sectors),
        out_shape=shape(FIELDS * end_rows, cells),
        in_specs=[VMEM],
        out_specs=VMEM,
    )(maps)
    for masks in groups(sectors):
        arrived = []
        for mask in masks:
            arrived.append(exchange(ends, sectors, mask))
        for values in arrived:
            ends = ends + values
    new_state = call(
        functools.partial(finish_kernel, sectors, levels),
        out_shape=shape(FIELDS, lines, cells),
        in_specs=[VMEM] * 5,
        out_specs=VMEM,
    )(ends, weights, flow, scan, sweep)
    return new_state.reshape(flow_state.shape)


def solution(mesh):
    return jax.shard_map(
        functools.partial(shards, mesh.shape["azim"], mesh.shape["row"]),
        mesh=mesh,
        in_specs=(
            P(None, None, "row", "azim"),
            P(None, None, "row", "azim"),
            P(None, "row", "azim"),
            P(),
            P(),
            P(None, None, None, "row", "azim"),
            P(None, None, None, "row", "azim"),
            P("row", "azim"),
            P("row", "azim"),
        ),
        out_specs=P(None, None, "row", "azim"),
        check_vma=False,
    )
```

```python
import functools

import jax
import jax.numpy as jnp
from jax import lax
from jax.experimental import pallas as pl
from jax.experimental.pallas import tpu as pltpu
from jax.sharding import PartitionSpec as P

FIELDS = 6
LANES = 128
HALF = 8
HALO = 72
JST_SECOND = 0.5
JST_FOURTH = 1.0 / 32.0
TIME_FACTOR = 1.5
VMEM = pl.BlockSpec(memory_space=pltpu.VMEM)
HBM = pl.BlockSpec(memory_space=pltpu.HBM)


def lane_ids():
    return lax.broadcasted_iota(jnp.int32, (HALF, LANES), 1)


def roll_lanes(x, shift):
    shift = shift % LANES
    return x if isinstance(shift, int) and shift == 0 else pltpu.roll(x, shift, 1)


def rows(half):
    return pl.ds(half * HALF, HALF)


def packing(sectors):
    return LANES // (2 * sectors)


def product(left, right):
    out = []
    for f in range(FIELDS):
        for h in range(FIELDS):
            acc = left[f * FIELDS] * right[h]
            for g in range(1, FIELDS):
                acc = acc + left[f * FIELDS + g] * right[g * FIELDS + h]
            out.append(acc)
    return out


def matvec(matrix, vector):
    out = []
    for f in range(FIELDS):
        acc = matrix[f * FIELDS] * vector[0]
        for g in range(1, FIELDS):
            acc = acc + matrix[f * FIELDS + g] * vector[g]
        out.append(acc)
    return out


def pack_last_lane(values, lane, base, width):
    acc = jnp.zeros((HALF, LANES), jnp.float32)
    for entry, pair in enumerate(values):
        for half in range(2):
            target = base + width * entry + half
            acc = jnp.where(lane == target, roll_lanes(pair[half], target + 1), acc)
    return acc


def groups(sectors):
    bits = sectors.bit_length() - 1
    found = []
    for low in reversed(range(0, bits - 1, 2)):
        found.append((1 << low, 2 << low, 3 << low))
    return found


def routes(sectors, place, cell):
    turn = (cell // LANES - place) & (sectors - 1)
    turns = (turn, (turn + 1) & (sectors - 1))
    flags = []
    half = sectors // 2
    for k in turns:
        borrow = jnp.where((place & (half - 1)) < (k & (half - 1)), half, 0)
        flags.append((k & half) ^ borrow)
    for unit, _, _ in groups(sectors):
        span = 4 * unit - 1
        mine = place & span & -unit
        for k in turns:
            low = (place - k) & (unit - 1)
            flags.append(mine ^ ((mine + low + k) & span & -unit))
        flags.append(mine ^ ((place - turn) & span & -unit))
    return flags


def edges_kernel(flow_in, flow, outlet, halo, sem):
    copy = pltpu.make_async_copy(flow_in, flow, sem)
    copy.start()
    lane = lane_ids()
    sub = lax.broadcasted_iota(jnp.int32, (HALF, LANES), 0)
    copy.wait()
    acc = jnp.zeros((HALF, LANES), jnp.float32)
    for f in range(FIELDS):
        lower, upper = flow[f, rows(0), :], flow[f, rows(1), :]
        outlet[pl.ds(f * HALF, HALF), :] = jnp.where((sub & 3) >= 2, lower, pltpu.roll(upper, HALF - 2, 0))
        for half, u in enumerate((lower, upper)):
            start = HALO + 4 * (2 * f + half)
            acc = jnp.where((lane >= start) & (lane < start + 2), roll_lanes(u, start), acc)
            acc = jnp.where((lane >= start + 2) & (lane < start + 4), roll_lanes(u, start + 4), acc)
    halo[...] = acc


def prepare_kernel(
    sectors,
    levels,
    flow,
    halo,
    old_in,
    step_in,
    azf_in,
    axf_in,
    inverse_in,
    lower_in,
    first_in,
    weight_in,
    gain,
    source,
    coef,
    flags,
    packed,
    scan,
    old,
    step_size,
    azf,
    axf,
    inverse,
    lower,
    first,
    weight,
    sems,
):
    copies = [
        pltpu.make_async_copy(src, dst, sems.at[at])
        for at, (src, dst) in enumerate(
            (
                (inverse_in, inverse),
                (lower_in, lower),
                (old_in, old),
                (step_in, step_size),
                (azf_in, azf),
                (axf_in, axf),
                (first_in, first),
                (weight_in, weight),
            )
        )
    ]
    for copy in copies:
        copy.start()
    lane = lane_ids()
    place = lax.axis_index("azim")
    for copy in copies:
        copy.wait()
    row = lax.broadcasted_iota(jnp.int32, (1, LANES), 1) * 0
    cell = row + jnp.broadcast_to(first[:, 0:1], (1, LANES))
    for at, flag in enumerate(routes(sectors, row + place, cell)):
        flags[pl.ds(at, 1), :] = flag
    flags[pl.ds(flags.shape[0] - 1, 1), :] = cell & (LANES - 1)
    for f in range(FIELDS):
        for g in range(FIELDS):
            at = f * FIELDS + g
            coef[pl.ds(at, 1), :] = jnp.broadcast_to(azf[f : f + 1, g : g + 1], (1, LANES))
            coef[pl.ds(36 + at, 1), :] = jnp.broadcast_to(axf[f : f + 1, g : g + 1], (1, LANES))
    coef[pl.ds(72, 1), :] = (weight[...].astype(jnp.float32) + 0.5) / 8.0
    for half in range(2):
        left = [inverse[e, rows(half), :] for e in range(36)]
        right = [lower[e, rows(half), :] for e in range(36)]
        for e, value in enumerate(product(left, right)):
            scan[e, rows(half), :] = value
    for half in range(2):
        minus_step = -step_size[rows(half), :]
        scaled = [minus_step * inverse[e, rows(half), :] for e in range(36)]
        change = [TIME_FACTOR * (flow[f, rows(half), :] - old[f, rows(half), :]) for f in range(FIELDS)]
        for e in range(36):
            gain[e, rows(half), :] = scaled[e]
        for f, value in enumerate(matvec(scaled, change)):
            source[f, rows(half), :] = value
    for level in range(levels):
        step = 1 << level
        keep = lane < step
        for half in range(2):
            later = [scan[36 * level + e, rows(half), :] for e in range(36)]
            earlier = [roll_lanes(x, step) for x in later]
            for e, value in enumerate(product(later, earlier)):
                scan[36 * (level + 1) + e, rows(half), :] = jnp.where(keep, later[e], value)
    acc = pack_last_lane(
        [[scan[36 * levels + e, rows(half), :] for half in range(2)] for e in range(36)], lane, 0, 2
    )
    packed[...] = jnp.where(lane < HALO, acc, halo[...])


def jst_parts(u0, um1, um2, up1, up2):
    p0, pm1, pm2, pp1, pp2 = [1.0 + x[0] * x[0] for x in (u0, um1, um2, up1, up2)]

    def sensor(up, mid, down):
        return jnp.abs(up - 2.0 * mid + down) / (up + 2.0 * mid + down)

    mid = sensor(pp1, p0, pm1)
    e2r = JST_SECOND * jnp.maximum(mid, sensor(pp2, pp1, p0))
    e2l = JST_SECOND * jnp.maximum(sensor(p0, pm1, pm2), mid)
    e4r = jnp.maximum(0.0, JST_FOURTH - e2r)
    e4l = jnp.maximum(0.0, JST_FOURTH - e2l)
    central, faces = [], []
    for f in range(FIELDS):
        dr = up1[f] - u0[f]
        dl = u0[f] - um1[f]
        third_r = up2[f] - 3.0 * up1[f] + 3.0 * u0[f] - um1[f]
        third_l = up1[f] - 3.0 * u0[f] + 3.0 * um1[f] - um2[f]
        central.append(0.5 * (up1[f] - um1[f]))
        faces.append((e2r * dr - e4r * third_r) - (e2l * dl - e4l * third_l))
    return central, faces


def gathered_at(sectors, difference):
    at, count = 0, 1
    for unit, _, _ in groups(sectors):
        at = at + ((difference // unit) & 3) * count
        count *= 4
    return at


def halo_at(sectors, difference):
    return 2 * gathered_at(sectors, difference) + difference // (sectors // 2)


def map_at(sectors, difference):
    return gathered_at(sectors, difference) + (difference // (sectors // 2)) * (sectors // 2)


def residual_kernel(sectors, ring_a, ring_b, ring, flow, coef, flags, reach, base, residual_out, packed):
    lane = lane_ids()
    sub = lax.broadcasted_iota(jnp.int32, (HALF, LANES), 0)
    place = lax.axis_index("azim")
    row = lax.axis_index("row")
    left_pack = ring[halo_at(sectors, place ^ ((place + sectors - 1) & (sectors - 1)))]
    right_pack = ring[halo_at(sectors, place ^ ((place + 1) & (sectors - 1)))]
    shift = flags[flags.shape[0] - 1, 0]
    back = (LANES - shift) & (LANES - 1)

    def coefficient(at):
        return jnp.broadcast_to(coef[pl.ds(at, 1), :], (HALF, LANES))

    frac = coefficient(72)
    ghost = []
    for f in range(FIELDS):
        a = pltpu.roll(ring_a[pl.ds(f * HALF, HALF), :], back, 1)
        b = pltpu.roll(ring_b[pl.ds(f * HALF, HALF), :], back, 1)
        one = jnp.where(lane < LANES - shift, a, b)
        two = pltpu.roll(jnp.where(lane == 0, b, one), LANES - 1, 1)
        ghost.append(frac * one + (1.0 - frac) * two)
    halo = jnp.where((lane & 3) < 2, right_pack, left_pack)
    axial = sub % 4
    ends = [[None, None] for _ in range(FIELDS)]
    is_first_row = row == 0
    for half in range(2):
        u0 = [flow[f, rows(half), :] for f in range(FIELDS)]
        um1, um2, up1, up2 = [], [], [], []
        for f in range(FIELDS):
            start = HALO + 4 * (2 * f + half)
            edge = roll_lanes(halo, LANES - 2 - start)
            um1.append(jnp.where(lane < 1, roll_lanes(halo, -(start + 3)), roll_lanes(u0[f], 1)))
            um2.append(jnp.where(lane < 2, edge, roll_lanes(u0[f], 2)))
            up1.append(jnp.where(lane >= LANES - 1, roll_lanes(halo, LANES - 1 - start), roll_lanes(u0[f], -1)))
            up2.append(jnp.where(lane >= LANES - 2, edge, roll_lanes(u0[f], -2)))
        az_central, az_faces = jst_parts(u0, um1, um2, up1, up2)
        um1, um2, up1, up2 = [], [], [], []
        for f in range(FIELDS):
            g = ghost[f]
            spread = pltpu.roll(g, HALF - 2, 0) if half == 0 else g
            u = u0[f]
            down1 = pltpu.roll(u, 1, 0)
            down2 = pltpu.roll(u, 2, 0)
            lift1 = pltpu.roll(u, HALF - 1, 0)
            lift2 = pltpu.roll(u, HALF - 2, 0)
            same = jnp.where(axial == 0, u, down1)
            spread = jnp.where(is_first_row, same, spread)
            next_ghost = pltpu.roll(spread, HALF - 1, 0)
            um1.append(jnp.where(axial == 0, next_ghost, down1))
            um2.append(jnp.where(axial < 2, spread, down2))
            last1 = jnp.where(axial == 3, u, lift1)
            up1.append(last1)
            up2.append(jnp.where(axial == 3, u, jnp.where(axial == 2, lift1, lift2)))
        ax_central, ax_faces = jst_parts(u0, um1, um2, up1, up2)
        residual = []
        for f in range(FIELDS):
            acc = -(az_faces[f] + ax_faces[f])
            for g in range(FIELDS):
                at = f * FIELDS + g
                acc = acc + coefficient(at) * az_central[g] + coefficient(36 + at) * ax_central[g]
            residual.append(acc)
        for f in range(FIELDS):
            residual_out[f, rows(half), :] = residual[f]
        parts = matvec([reach[e, rows(half), :] for e in range(36)], residual)
        for f in range(FIELDS):
            ends[f][half] = jnp.sum(parts[f], axis=1, keepdims=True)
    per = packing(sectors)
    for first in range(0, FIELDS, per):
        acc = base[pl.ds(HALF * (first // per), HALF), :]
        for entry, pair in enumerate(ends[first : first + per]):
            for half in range(2):
                target = entry * 2 * sectors + half
                acc = jnp.where(lane == target, acc + jnp.broadcast_to(pair[half], (HALF, LANES)), acc)
        packed[pl.ds(HALF * (first // per), HALF), :] = roll_lanes(acc, 2 * place)


def reach_kernel(sectors, levels, scan, gain, source, reach, base, work):
    lane = lane_ids()
    one = [jnp.float32(1.0 if e % 7 == 0 else 0.0) for e in range(36)]
    for half in range(2):
        for e in range(36):
            work[e, rows(half), :] = scan[e, rows(half), :]
    for level in range(levels):
        step = 1 << level
        for half in range(2):
            here = [work[e, rows(half), :] for e in range(36)]
            later = [
                jnp.where(lane < LANES - step, roll_lanes(x, -step), one[e]) for e, x in enumerate(here)
            ]
            for e, value in enumerate(product(later, here)):
                work[e, rows(half), :] = value
    sums = [[None, None] for _ in range(FIELDS)]
    for half in range(2):
        after = [
            jnp.where(lane < LANES - 1, roll_lanes(work[e, rows(half), :], -1), one[e]) for e in range(36)
        ]
        for e, value in enumerate(product(after, [gain[e, rows(half), :] for e in range(36)])):
            reach[e, rows(half), :] = value
        for f, value in enumerate(matvec(after, [source[f, rows(half), :] for f in range(FIELDS)])):
            sums[f][half] = jnp.sum(value, axis=1, keepdims=True)
    per = packing(sectors)
    for first in range(0, FIELDS, per):
        acc = jnp.zeros((HALF, LANES), jnp.float32)
        for entry, pair in enumerate(sums[first : first + per]):
            for half in range(2):
                target = entry * 2 * sectors + half
                acc = jnp.where(lane == target, jnp.broadcast_to(pair[half], (HALF, LANES)), acc)
        base[pl.ds(HALF * (first // per), HALF), :] = acc


def sweep_kernel(levels, residual, gain, source, scan, sweep):
    lane = lane_ids()
    values = [[None, None] for _ in range(FIELDS)]
    for half in range(2):
        added = matvec(
            [gain[e, rows(half), :] for e in range(36)], [residual[f, rows(half), :] for f in range(FIELDS)]
        )
        for f in range(FIELDS):
            values[f][half] = source[f, rows(half), :] + added[f]
    for level in range(levels):
        step = 1 << level
        for half in range(2):
            before = [jnp.where(lane < step, 0.0, roll_lanes(values[f][half], step)) for f in range(FIELDS)]
            matrix = [scan[36 * level + e, rows(half), :] for e in range(36)]
            for f, gained in enumerate(matvec(matrix, before)):
                values[f][half] = values[f][half] + gained
    for f in range(FIELDS):
        for half in range(2):
            sweep[f, rows(half), :] = values[f][half]


def closing_kernel(sectors, ring, weights):
    lane = lane_ids()
    place = lax.axis_index("azim")
    width = 2 * sectors
    one = [jnp.float32(1.0 if e % 7 == 0 else 0.0) for e in range(36)]
    turned = []
    for t in range(sectors):
        at = map_at(sectors, place ^ ((place + t) & (sectors - 1)))
        turned.append(roll_lanes(ring[at], 2 * t))
    pair = lane >> 1
    maps = []
    for e in range(36):
        acc = turned[0]
        for t in range(1, sectors):
            acc = jnp.where(pair == (e + t) % (LANES // 2), turned[t], acc)
        maps.append(roll_lanes(acc, -2 * e))
    step = 2
    while step < width:
        later = [jnp.where(lane < width - step, roll_lanes(x, -step), one[e]) for e, x in enumerate(maps)]
        maps = product(later, maps)
        step *= 2
    suffix = [jnp.where(lane < width - 2, roll_lanes(maps[e], -2), one[e]) for e in range(36)]
    system = [[one[f * 6 + g] - maps[f * 6 + g] for g in range(6)] for f in range(6)]
    result = [[jnp.full((HALF, LANES), one[f * 6 + g]) for g in range(6)] for f in range(6)]
    for pivot in range(6):
        scale = 1.0 / system[pivot][pivot]
        for g in range(pivot + 1, 6):
            system[pivot][g] = system[pivot][g] * scale
        for g in range(pivot + 1):
            result[pivot][g] = result[pivot][g] * scale
        for f in range(6):
            if f == pivot:
                continue
            factor = system[f][pivot]
            for g in range(pivot + 1, 6):
                system[f][g] = system[f][g] - factor * system[pivot][g]
            for g in range(pivot + 1):
                result[f][g] = result[f][g] - factor * result[pivot][g]
    closing = []
    for e in range(36):
        value = jnp.where(lane < 2, result[e // 6][e % 6], 0.0)
        step = 2
        while step < width:
            value = value + roll_lanes(value, step)
            step *= 2
        closing.append(value)
    start = product(closing, suffix)
    per = packing(sectors)
    turn = 2 * place
    crossed = (lane & (width - 1)) < turn
    for f in range(FIELDS):
        for first in range(0, FIELDS, per):
            acc = jnp.zeros((HALF, LANES), jnp.float32)
            for entry in range(min(per, FIELDS - first)):
                at = entry * width
                inside = (lane >= at) & (lane < at + width)
                acc = jnp.where(inside, roll_lanes(start[f * 6 + first + entry], at), acc)
            ahead = pltpu.roll(acc, turn, 1)
            behind = pltpu.roll(acc, lax.rem(LANES + turn - width, LANES), 1)
            row = HALF * (f * pl.cdiv(FIELDS, per) + first // per)
            weights[pl.ds(row, HALF), :] = jnp.where(crossed, behind, ahead)


def finish_kernel(sectors, levels, gathered, weights, flow, scan, sweep, out, held, sems):
    lane = lane_ids()
    count = pl.cdiv(FIELDS, packing(sectors))
    begin = [[None] * FIELDS for _ in range(2)]
    for f in range(FIELDS):
        acc = None
        for at in range(count):
            term = weights[pl.ds(HALF * (f * count + at), HALF), :] * gathered[pl.ds(HALF * at, HALF), :]
            acc = term if acc is None else acc + term
        for half in range(2):
            total = jnp.sum(jnp.where((lane & 1) == half, acc, 0.0), axis=1, keepdims=True)
            begin[half][f] = jnp.broadcast_to(total, (HALF, LANES))
    copies = []
    for half in range(2):
        gained = matvec([scan[36 * levels + e, rows(half), :] for e in range(36)], begin[half])
        for f in range(FIELDS):
            held[half, f] = flow[f, rows(half), :] + (gained[f] + sweep[f, rows(half), :])
        copies.append(pltpu.make_async_copy(held.at[half], out.at[:, rows(half), :], sems.at[half]))
        copies[-1].start()
    for copy in copies:
        copy.wait()


def exchange(values, sectors, mask):
    return lax.ppermute(values, "azim", [(i, i ^ mask) for i in range(sectors)])


def from_upstream(values, sectors, row_count, mask):
    return lax.ppermute(
        values,
        ("azim", "row"),
        [
            (i * row_count + r, (i ^ mask) * row_count + (r + 1) % row_count)
            for i in range(sectors)
            for r in range(row_count)
        ],
    )


def in_hbm(x):
    return pltpu.with_memory_space_constraint(x, pltpu.HBM)


def shape(*dims):
    return jax.ShapeDtypeStruct(dims, jnp.float32)


def shards(
    sectors,
    row_count,
    flow_state,
    old_state,
    local_step,
    azim_flux,
    axial_flux,
    block_inverse,
    lower_block,
    intersection_first,
    intersection_weight,
):
    radial, axial, cells = flow_state.shape[1:]
    lines = radial * axial
    levels = cells.bit_length() - 1
    end_rows = HALF * pl.cdiv(FIELDS, packing(sectors))
    flag_rows = HALF * pl.cdiv(3 * sectors.bit_length(), HALF)
    count = FIELDS * HALF
    call = functools.partial(
        pl.pallas_call, compiler_params=pltpu.CompilerParams(vmem_limit_bytes=16 << 20)
    )

    flow, outlet, halo = call(
        edges_kernel,
        out_shape=(shape(FIELDS, lines, cells), shape(count, cells), shape(HALF, cells)),
        in_specs=[HBM],
        out_specs=(VMEM,) * 3,
        scratch_shapes=[pltpu.SemaphoreType.DMA(())],
    )(in_hbm(flow_state.reshape(FIELDS, lines, cells)))
    top = sectors // 2
    upstream_far = from_upstream(outlet, sectors, row_count, top)
    halo_far = exchange(halo, sectors, top)
    upstream = from_upstream(outlet, sectors, row_count, 0)
    gain, source, coef, flags, packed, scan = call(
        functools.partial(prepare_kernel, sectors, levels),
        out_shape=(
            shape(36, lines, cells),
            shape(FIELDS, lines, cells),
            shape(80, cells),
            jax.ShapeDtypeStruct((flag_rows, cells), jnp.int32),
            shape(HALF, cells),
            shape(36 * (levels + 1), lines, cells),
        ),
        in_specs=[VMEM] * 2 + [HBM] * 8,
        out_specs=(VMEM,) * 6,
        scratch_shapes=[
            pltpu.VMEM((FIELDS, lines, cells), jnp.float32),
            pltpu.VMEM((lines, cells), jnp.float32),
            pltpu.VMEM((FIELDS, FIELDS), jnp.float32),
            pltpu.VMEM((FIELDS, FIELDS), jnp.float32),
            pltpu.VMEM((36, lines, cells), jnp.float32),
            pltpu.VMEM((36, lines, cells), jnp.float32),
            pltpu.VMEM((1, cells), jnp.int32),
            pltpu.VMEM((1, cells), jnp.int32),
            pltpu.SemaphoreType.DMA((8,)),
        ],
    )(
        flow,
        halo,
        *(
            in_hbm(x)
            for x in (
                old_state.reshape(FIELDS, lines, cells),
                local_step.reshape(lines, cells),
                azim_flux,
                axial_flux,
                block_inverse.reshape(36, lines, cells),
                lower_block.reshape(36, lines, cells),
                intersection_first,
                intersection_weight,
            )
        ),
    )
    ring_a = jnp.where(flags[0:1] != 0, upstream_far, upstream)
    ring_b = jnp.where(flags[1:2] != 0, upstream_far, upstream)
    ring = jnp.concatenate([packed, halo_far], axis=0)
    at = 2
    for masks in groups(sectors):
        on_a, on_b, to_a = (flags[at + k : at + k + 1] for k in range(3))
        near_packs = ring.reshape(-1, 2, HALF, cells)[:, 0]
        arrived = []
        for mask in masks:
            slim = mask in (1, 2)
            packs = near_packs.reshape(-1, cells) if slim else ring
            sent = jnp.concatenate([jnp.where(to_a == mask, ring_a, ring_b), packs], axis=0)
            values = exchange(sent, sectors, mask)
            if slim:
                got = values[count:].reshape(near_packs.shape)
                both = jnp.stack([got, jnp.zeros_like(got)], axis=1).reshape(-1, cells)
                values = jnp.concatenate([values[:count], both], axis=0)
            arrived.append(values)
        for mask, values in zip(masks, arrived):
            ring_a = jnp.where(on_a == mask, values[:count], ring_a)
            ring_b = jnp.where(on_b == mask, values[:count], ring_b)
        ring = jnp.concatenate([ring] + [values[count:] for values in arrived], axis=0)
        at += 3
    ring = ring.reshape(top, 2, HALF, cells)
    halos = ring.reshape(sectors, HALF, cells)

    reach, base = call(
        functools.partial(reach_kernel, sectors, levels),
        out_shape=(shape(36, lines, cells), shape(end_rows, cells)),
        in_specs=[VMEM] * 3,
        out_specs=(VMEM, VMEM),
        scratch_shapes=[pltpu.VMEM((36, lines, cells), jnp.float32)],
    )(scan, gain, source)
    residual, ends = call(
        functools.partial(residual_kernel, sectors),
        out_shape=(shape(FIELDS, lines, cells), shape(end_rows, cells)),
        in_specs=[VMEM] * 8,
        out_specs=(VMEM, VMEM),
    )(ring_a, ring_b, halos, flow, coef, flags, reach, base)
    sweep = call(
        functools.partial(sweep_kernel, levels),
        out_shape=shape(FIELDS, lines, cells),
        in_specs=[VMEM] * 4,
        out_specs=VMEM,
        cost_estimate=pl.CostEstimate(flops=1 << 20, bytes_accessed=1 << 21, transcendentals=0),
    )(residual, gain, source, scan)
    values = exchange(jnp.concatenate([ends, ring[:, 0].reshape(top * HALF, cells)], axis=0), sectors, top)
    ends = ends + values[:end_rows]
    maps = jnp.concatenate([ring[:, 0], values[end_rows:].reshape(top, HALF, cells)], axis=0)
    weights = call(
        functools.partial(closing_kernel, sectors),
        out_shape=shape(FIELDS * end_rows, cells),
        in_specs=[VMEM],
        out_specs=VMEM,
    )(maps)
    for masks in groups(sectors):
        for values in [exchange(ends, sectors, mask) for mask in masks]:
            ends = ends + values
    new_state = call(
        functools.partial(finish_kernel, sectors, levels),
        out_shape=shape(FIELDS, lines, cells),
        in_specs=[VMEM] * 5,
        out_specs=HBM,
        scratch_shapes=[
            pltpu.VMEM((2, FIELDS, HALF, cells), jnp.float32),
            pltpu.SemaphoreType.DMA((2,)),
        ],
    )(ends, weights, flow, scan, sweep)
    return new_state.reshape(flow_state.shape)


def solution(mesh):
    return jax.shard_map(
        functools.partial(shards, mesh.shape["azim"], mesh.shape["row"]),
        mesh=mesh,
        in_specs=(
            P(None, None, "row", "azim"),
            P(None, None, "row", "azim"),
            P(None, "row", "azim"),
            P(),
            P(),
            P(None, None, None, "row", "azim"),
            P(None, None, None, "row", "azim"),
            P("row", "azim"),
            P("row", "azim"),
        ),
        out_specs=P(None, None, "row", "azim"),
        check_vma=False,
    )
```
